256 devices in a mesh: rows: 8 (over y, x_lo), cols: 32 (over x_hi, z, core).
Axes of the slice: x: 4 (x_hi: 2, x_lo: 2; x = x_hi * 2 + x_lo), y: 4, z: 8, core: 2. Of those that a mesh axis runs over, the one named last changes fastest.
Arguments:
- interaction: bfloat16 [16384, 8192], P('rows', 'cols'), may hold values from -0.125 to 0.125
- commands: bfloat16 [1024, 8192], P('rows', 'cols'), may hold values from -6 to 6
- slopes_measured: bfloat16 [16384, 1024], P(('rows', 'cols')), may hold values from -6 to 6
- frame_lag: int32 [1], replicated, may hold values from 1 to 256
- frame_count: int32 [1], replicated, may hold values from 256 to 1024
Outputs:
- lag_covariance: float32 [16384, 16384], P('rows', 'cols')
The draws below stay inside these ranges and needn't reach their ends.
All inputs are finite; a program needn't handle non-finite values.
Results may differ from the reference program's by a relative error of at most 0.004.
Values may be sent and summed in bfloat16 or wider, within the bound.
A program may use at most 64 MiB of HBM per device.

```python
import math
import jax
import jax.numpy as jnp
from jax import lax

SLOPES = 16384
ACTUATORS = 8192
FRAMES = 1024


def spiked(values, stream_key, source, target, blocks, factor):
    def block_of(dim):
        return (jnp.arange(values.shape[dim]) // (values.shape[dim] // blocks)).reshape((-1,) + (1,) * (values.ndim - 1 - dim))

    near = jax.random.permutation(stream_key, blocks)[block_of(target)]
    second = (block_of(target) + blocks // 2) % blocks
    return jnp.where((block_of(source) == near) | (block_of(source) == second), factor * values, values)


def block_levels(own_key, dims, split, least, top_value):
    loudness = 1.0
    for dim, blocks in split:
        heights = jax.random.uniform(jax.random.fold_in(jax.random.fold_in(own_key, 6), dim), (blocks,), jnp.float32, least / len(split), top_value / len(split))
        loudness = loudness * jnp.repeat(jnp.exp(heights), dims[dim] // blocks).reshape((-1,) + (1,) * (len(dims) - 1 - dim))
    return loudness


def bell_draw(own_key, dims, spread, most, cuts=(), kind=jnp.bfloat16):
    gain = block_levels(own_key, dims, cuts, -0.22, 0.18) if cuts else 1.0
    result = jax.random.normal(own_key, dims, jnp.float32) * spread * gain
    return jnp.minimum(jnp.maximum(result, -most), most).astype(kind)


def gaussian_with(key, dims, width, bound, split, heavy, kind=jnp.bfloat16):
    values = width * jax.random.normal(key, dims, jnp.float32)
    if split:
        values = values * block_levels(key, dims, split, -0.22, 0.18)
    return jnp.clip(spiked(values, jax.random.fold_in(key, 3), *heavy), -bound, bound).astype(kind)


def setup_inputs(seed: int = 0) -> dict:
    splits = jax.random.split(jax.random.key(seed), 6)
    return {
        "interaction": gaussian_with(splits[0], (SLOPES, ACTUATORS), ACTUATORS ** -0.5, 0.125, ((0, 8), (1, 32)), (1, 0, 32, 2.75)),
        "commands": bell_draw(splits[1], (FRAMES, ACTUATORS), 1.0, 6.0, ((0, 8), (1, 32))),
        "slopes_measured": bell_draw(splits[2], (SLOPES, FRAMES), 1.0, 6.0, ((0, 256),)),
        "frame_lag": jax.random.randint(splits[3], (1,), 1, FRAMES // 4 + 1).astype(jnp.int32),
        "frame_count": jax.random.randint(splits[4], (1,), FRAMES // 4, FRAMES + 1).astype(jnp.int32),
    }


def reference(interaction, commands, slopes_measured, frame_lag, frame_count):
    margin = FRAMES // 4
    padded = jnp.concatenate([jnp.zeros((margin, ACTUATORS), commands.dtype), commands], axis=0)
    delayed = lax.dynamic_slice_in_dim(padded, (margin - frame_lag[0]).astype(jnp.int32), FRAMES, 0)
    response = jnp.dot(interaction, delayed.T, preferred_element_type=jnp.float32)
    summed = response + slopes_measured.astype(jnp.float32)
    frame_index = jnp.arange(FRAMES, dtype=jnp.int32)
    openloop = jnp.where(frame_index[None, :] < frame_count[0], summed, 0.0).astype(jnp.bfloat16)
    advanced = jnp.concatenate([openloop[:, 1:], jnp.zeros((SLOPES, 1), jnp.bfloat16)], axis=1)
    scaling = 1.0 / math.sqrt(FRAMES)
    return jnp.dot(advanced, openloop.T, preferred_element_type=jnp.float32) * scaling
```

```python
import math

import jax
import jax.numpy as jnp
from jax import lax
from jax.experimental import pallas as pl
from jax.experimental.pallas import tpu as pltpu
from jax.sharding import PartitionSpec as P

FRAMES = 1024
CHUNK = 256
CHUNKS = FRAMES // CHUNK
BF, F32 = jnp.bfloat16, jnp.float32
VMEM = pl.BlockSpec(memory_space=pltpu.VMEM)
Y_ORDER = (0, 1, 3, 2)
HOPS = {"L": (BF, BF, F32, F32), "S": (BF, BF, F32)}


class Place:
    def __init__(self):
        self.r = lax.axis_index("rows")
        self.c = lax.axis_index("cols")
        self.y, self.xl = self.r // 2, self.r % 2
        self.xh, self.z, self.core = self.c // 16, (self.c // 2) % 8, self.c % 2
        self.sign = 1 - 2 * self.core

    def col(self, xh, z, core):
        return xh * 16 + z * 2 + core

    def at_z(self, dz):
        return self.r, self.col(self.xh, (self.z + dz + 16) % 8, self.core)

    def at_y(self, dy):
        return (self.r + 2 * dy + 8) % 8, self.c

    def x_far(self):
        return self.r, (self.c + 16) % 32

    def x_near(self):
        return self.y * 2 + (1 - self.xl), self.c

    def other_core(self):
        return self.r, self.c + self.sign


class Net:
    def __init__(self, send_sem, recv_sem):
        self.send_sem, self.recv_sem = send_sem, recv_sem
        self.copies = {}

    def send(self, key, src, dst, device):
        n = len(self.copies)
        copy = pltpu.make_async_remote_copy(
            src_ref=src,
            dst_ref=dst,
            send_sem=self.send_sem.at[n],
            recv_sem=self.recv_sem.at[n],
            device_id=device,
            device_id_type=pl.DeviceIdType.MESH,
        )
        copy.start()
        self.copies[key] = [copy, False]

    def wait(self, key):
        entry = self.copies[key]
        assert not entry[1]
        entry[0].wait_recv()
        entry[1] = True

    def finish(self):
        for copy, received in self.copies.values():
            assert received
            copy.wait_send()


def greet(devices):
    barrier = pltpu.get_barrier_semaphore()
    for device in devices:
        pl.semaphore_signal(barrier, inc=1, device_id=device, device_id_type=pl.DeviceIdType.MESH)
    pl.semaphore_wait(barrier, len(devices))


def reduce_kernel(a_ref, d_ref, r_ref, a2, dg, p, sb, rb, sf, rf, fin, xr, send_sem, recv_sem):
    me = Place()
    r, z, sign = me.r, me.z, me.sign
    greet(
        [me.other_core(), me.x_near(), me.x_far(), me.at_z(1), me.at_z(-1)]
        + [me.at_y(d) for d in (1, 2, 3)]
    )
    net = Net(send_sem, recv_sem)
    near = me.y * 2 + (1 - me.xl)
    net.send("d_near", d_ref, dg.at[0, r], me.x_near())
    net.send("d_core", d_ref, dg.at[1, r], me.other_core())
    net.send("a", a_ref.at[:, :, 1 - me.core], a2, me.other_core())
    for o in Y_ORDER[1:]:
        net.send(("d_y", o), d_ref, dg.at[0, r], me.at_y(-o))
    dg[0, r] = d_ref[...]
    net.wait("d_near")
    net.send("d_near_core", dg.at[0, near], dg.at[1, near], me.other_core())
    for o in Y_ORDER[1:]:
        net.send(("d_near_y", o), dg.at[0, near], dg.at[0, near], me.at_y(-o))

    def y_of(f):
        return (me.y + Y_ORDER[f]) % 4

    def product(f):
        o = Y_ORDER[f]
        if f == 0:
            net.wait("d_core")
            net.wait("a")
            net.wait("d_near_core")
        else:
            net.wait(("d_y", o))
            net.wait(("d_near_y", o))
            two = pl.ds(y_of(f) * 2, 2)
            net.send(("d_y_core", o), dg.at[0, two], dg.at[1, two], me.other_core())
            net.wait(("d_y_core", o))
        mine = dg[0, pl.ds(y_of(f) * 2, 2)].reshape(CHUNK, 256)
        others = dg[1, pl.ds(y_of(f) * 2, 2)].reshape(CHUNK, 256)
        contract = (((1,), (1,)), ((), ()))
        for xh in range(2):
            own = lax.dot_general(
                a_ref[xh, :, me.core].reshape(512, 256), mine, contract, preferred_element_type=F32
            )
            rest = lax.dot_general(
                a2[xh].reshape(512, 256), others, contract, preferred_element_type=F32
            )
            p[f, xh] = (own + rest).reshape(8, 64, CHUNK)

    slots = {}
    for way, kinds in HOPS.items():
        for hop, kind in enumerate(kinds, 1):
            slots[way, hop] = (kind, sum(1 for k, _ in slots.values() if k is kind))

    def buffer(f, way, hop, sending):
        kind, n = slots[way, hop]
        if kind is BF:
            return (sb if sending else rb).at[f, n]
        return (sf if sending else rf).at[f, n]

    def hop_on(f, way, hop):
        hops = len(HOPS[way])
        step = sign if way == "L" else -sign
        owner = (z + step * (hops + 1 - hop) + 16) % 8
        value = p[f, :, owner]
        if hop > 1:
            net.wait((f, way, hop - 1))
            value += buffer(f, way, hop - 1, False)[...].astype(F32)
        out = buffer(f, way, hop, True)
        out[...] = value.astype(HOPS[way][hop - 1])
        net.send((f, way, hop), out, buffer(f, way, hop, False), me.at_z(step))

    def total(f):
        value = p[f, :, z]
        for way in HOPS:
            net.wait((f, way, len(HOPS[way])))
            value += buffer(f, way, len(HOPS[way]), False)[...]
        fin[f] = value
        net.send((f, "x"), fin.at[f, 1 - me.xh], xr.at[f], me.x_far())

    def store(f):
        net.wait((f, "x"))
        r_ref[:, pl.ds(pl.multiple_of(y_of(f) * CHUNK, CHUNK), CHUNK)] = fin[f, me.xh] + xr[f]

    for turn in range(CHUNKS + 5):
        for f in range(CHUNKS):
            stage = turn - f
            if stage == 0:
                product(f)
                hop_on(f, "L", 1)
                hop_on(f, "S", 1)
            elif stage in (1, 2, 3):
                hop_on(f, "L", stage + 1)
                if stage < 3:
                    hop_on(f, "S", stage + 1)
            elif stage == 4:
                total(f)
            elif stage == 5:
                store(f)
    net.finish()


def gather_kernel(o_ref, osh_ref, rows_ref, cols_ref, send_sem, recv_sem):
    me = Place()
    r, c, z, xh = me.r, me.c, me.z, me.xh
    target = ((c + 4) % 8, r * 4 + c // 8)
    source = (c // 4, (c % 4) * 8 + (r + 4) % 8)
    greet(
        [me.other_core(), me.x_near(), me.x_far(), me.at_z(1), me.at_z(-1), me.at_y(1), me.at_y(-1)]
        + [target, source]
    )
    net = Net(send_sem, recv_sem)
    first, second = pl.ds(0, 32), pl.ds(32, 32)
    hops = {"L": 4, "S": 3}
    step = {"L": me.sign, "S": -me.sign}

    def slot(other, dz):
        return me.col((1 - xh) if other else xh, (z + dz + 16) % 8, me.core)

    def pass_on(key, n, half, device):
        piece = rows_ref.at[n, half]
        net.send(key, piece, piece, device)

    net.send("x1", o_ref.at[first], rows_ref.at[c, first], me.x_far())
    net.send("permute", osh_ref, cols_ref.at[c % 8], target)
    for way in hops:
        net.send(("z2", way, 1), o_ref.at[second], rows_ref.at[c, second], me.at_z(step[way]))
    for way in hops:
        net.send(("z1", way, 1), o_ref.at[first], rows_ref.at[c, first], me.at_z(step[way]))
    net.send(("x2", "own", 0), o_ref.at[second], rows_ref.at[c, second], me.x_far())
    net.send("core_own", o_ref, rows_ref.at[c], me.other_core())
    rows_ref[c] = o_ref[...]
    net.wait("x1")
    for way in hops:
        pass_on(("z1p", way, 1), slot(True, 0), first, me.at_z(step[way]))

    def to_core(key, n):
        net.send(key, rows_ref.at[n], rows_ref.at[n], me.other_core())

    def col_slot(row):
        return (row + 4) % 8

    def pass_col(key, row, device):
        piece = cols_ref.at[col_slot(row)]
        net.send(key, piece, piece, device)

    near = me.y * 2 + (1 - me.xl)
    for t in range(1, 5):
        for way in hops:
            if t > hops[way]:
                continue
            n, m = slot(False, -step[way] * t), slot(True, -step[way] * t)
            ahead = me.at_z(step[way])
            net.wait(("z2", way, t))
            if t < hops[way]:
                pass_on(("z2", way, t + 1), n, second, ahead)
            pass_on(("x2", way, t), n, second, me.x_far())
            net.wait(("z1", way, t))
            if t < hops[way]:
                pass_on(("z1", way, t + 1), n, first, ahead)
            to_core(("core", way, t), n)
            net.wait(("z1p", way, t))
            if t < hops[way]:
                pass_on(("z1p", way, t + 1), m, first, ahead)
        if t == 1:
            net.wait("permute")
            pass_col("near", r, me.x_near())
            pass_col(("y0", 1), r, me.at_y(1))
            pass_col(("y0", -1), r, me.at_y(-1))
        if t == 2:
            net.wait("near")
            pass_col(("y1", 1), near, me.at_y(1))
            pass_col(("y1", -1), near, me.at_y(-1))
        if t == 3:
            net.wait(("y0", 1))
            pass_col(("y2", 1), (r + 6) % 8, me.at_y(1))
            net.wait(("y1", -1))
            pass_col(("y2", -1), (near + 2) % 8, me.at_y(-1))
    net.wait(("x2", "own", 0))
    to_core(("core_far", "own", 0), slot(True, 0))
    for t in range(1, 5):
        for way in hops:
            if t <= hops[way]:
                net.wait(("x2", way, t))
                to_core(("core_far", way, t), slot(True, -step[way] * t))
    for key in [("y0", -1), ("y1", 1), ("y2", 1), ("y2", -1), "core_own"]:
        net.wait(key)
    for key, entry in net.copies.items():
        if not entry[1]:
            net.wait(key)
    net.finish()


def reduced(interaction, commands):
    kinds = [kind for way in HOPS.values() for kind in way]
    n_bf, n_f32 = kinds.count(BF), kinds.count(F32)
    piece = (2, 64, CHUNK)
    copies = 6 + 3 * (len(Y_ORDER) - 1) + CHUNKS * (len(kinds) + 1)
    return pl.pallas_call(
        reduce_kernel,
        out_shape=jax.ShapeDtypeStruct((64, FRAMES), F32),
        in_specs=[VMEM] * 2,
        out_specs=VMEM,
        scratch_shapes=[
            pltpu.VMEM((2, 8, 64, 256), BF),
            pltpu.VMEM((2, 8, 128, 256), BF),
            pltpu.VMEM((CHUNKS, 2, 8, 64, CHUNK), F32),
            pltpu.VMEM((CHUNKS, n_bf) + piece, BF),
            pltpu.VMEM((CHUNKS, n_bf) + piece, BF),
            pltpu.VMEM((CHUNKS, n_f32) + piece, F32),
            pltpu.VMEM((CHUNKS, n_f32) + piece, F32),
            pltpu.VMEM((CHUNKS,) + piece, F32),
            pltpu.VMEM((CHUNKS, 64, CHUNK), F32),
            pltpu.SemaphoreType.DMA((copies,)),
            pltpu.SemaphoreType.DMA((copies,)),
        ],
        compiler_params=pltpu.CompilerParams(collective_id=0, has_side_effects=True),
        name="reduce_slopes",
    )(interaction.reshape(2, 8, 2, 64, 256), commands)


def gathered(openloop, shifted):
    return pl.pallas_call(
        gather_kernel,
        out_shape=(
            jax.ShapeDtypeStruct((32, 64, FRAMES), BF),
            jax.ShapeDtypeStruct((8, 64, FRAMES), BF),
        ),
        in_specs=[VMEM] * 2,
        out_specs=(VMEM, VMEM),
        scratch_shapes=[pltpu.SemaphoreType.DMA((80,)), pltpu.SemaphoreType.DMA((80,))],
        compiler_params=pltpu.CompilerParams(collective_id=1, has_side_effects=True),
        name="gather_slopes",
    )(openloop, shifted)


def delay_frames(response, frame_lag):
    margin = FRAMES // 4
    padded = jnp.concatenate(
        [jnp.zeros((response.shape[0], margin), response.dtype), response], axis=1
    )
    return lax.dynamic_slice_in_dim(padded, margin - frame_lag[0], FRAMES, 1)


def mask_frames(summed, frame_count):
    frame_index = lax.broadcasted_iota(jnp.int32, summed.shape, 1)
    return jnp.where(frame_index < frame_count[0], summed, 0.0).astype(BF)


def local(interaction, commands, slopes_measured, frame_lag, frame_count):
    response = reduced(interaction, commands)
    summed = delay_frames(response, frame_lag) + slopes_measured.astype(F32)
    openloop = mask_frames(summed, frame_count)
    shifted = jnp.concatenate([jnp.zeros((64, 1), BF), openloop[:, :-1]], axis=1)
    rows, cols = gathered(openloop, shifted)
    tile = lax.dot_general(
        rows.reshape(2048, FRAMES),
        cols.reshape(512, FRAMES),
        (((1,), (1,)), ((), ())),
        preferred_element_type=F32,
    )
    return tile * (1.0 / math.sqrt(FRAMES))


def solution(mesh):
    return jax.shard_map(
        local,
        mesh=mesh,
        in_specs=(P("rows", "cols"), P("rows", "cols"), P(("rows", "cols"), None), P(), P()),
        out_specs=P("rows", "cols"),
        check_vma=False,
    )
```

```python
import math

import jax
import jax.numpy as jnp
from jax import lax
from jax.experimental import pallas as pl
from jax.experimental.pallas import tpu as pltpu
from jax.sharding import PartitionSpec as P

FRAMES = 1024
CHUNK = 256
CHUNKS = FRAMES // CHUNK
BF, F32 = jnp.bfloat16, jnp.float32
VMEM = pl.BlockSpec(memory_space=pltpu.VMEM)
Y_ORDER = (0, 1, 3, 2)
HOPS = {"L": (BF, BF, F32, F32), "S": (BF, BF, F32)}
A_ORDER = (("L", 1), ("S", 1), ("L", 2), ("S", 2), ("L", 3), ("S", 3), ("L", 4), ("L", 5))


class Place:
    def __init__(self):
        self.r = lax.axis_index("rows")
        self.c = lax.axis_index("cols")
        self.y, self.xl = self.r // 2, self.r % 2
        self.xh, self.z, self.core = self.c // 16, (self.c // 2) % 8, self.c % 2
        self.sign = 1 - 2 * self.core

    def col(self, xh, z, core):
        return xh * 16 + z * 2 + core

    def at_z(self, dz):
        return self.r, self.col(self.xh, (self.z + dz + 16) % 8, self.core)

    def at_y(self, dy):
        return (self.r + 2 * dy + 8) % 8, self.c

    def x_far(self):
        return self.r, (self.c + 16) % 32

    def x_far_core(self):
        return self.r, self.col(1 - self.xh, self.z, 1 - self.core)

    def x_cross(self):
        return self.y * 2 + (1 - self.xl), (self.c + 16) % 32

    def x_near(self):
        return self.y * 2 + (1 - self.xl), self.c

    def other_core(self):
        return self.r, self.c + self.sign


class Net:
    def __init__(self, send_sem, recv_sem):
        self.send_sem, self.recv_sem = send_sem, recv_sem
        self.copies = {}

    def send(self, key, src, dst, device):
        n = len(self.copies)
        copy = pltpu.make_async_remote_copy(
            src_ref=src,
            dst_ref=dst,
            send_sem=self.send_sem.at[n],
            recv_sem=self.recv_sem.at[n],
            device_id=device,
            device_id_type=pl.DeviceIdType.MESH,
        )
        copy.start()
        self.copies[key] = [copy, False]

    def wait(self, key):
        entry = self.copies[key]
        assert not entry[1]
        entry[0].wait_recv()
        entry[1] = True

    def finish(self):
        for copy, received in self.copies.values():
            assert received
            copy.wait_send()


def greet(devices):
    barrier = pltpu.get_barrier_semaphore()
    for device in devices:
        pl.semaphore_signal(barrier, inc=1, device_id=device, device_id_type=pl.DeviceIdType.MESH)
    pl.semaphore_wait(barrier, len(devices))


def reduce_kernel(a_ref, d_ref, r_ref, a4, dg, sb, rb, sf, rf, send_sem, recv_sem):
    me = Place()
    r, z, xh, core, sign = me.r, me.z, me.xh, me.core, me.sign
    greet(
        [me.other_core(), me.x_near(), me.x_far(), me.x_cross(), me.x_far_core(), me.at_z(1), me.at_z(-1)]
        + [me.at_y(1), me.at_y(-1)]
    )
    net = Net(send_sem, recv_sem)
    near = me.y * 2 + (1 - me.xl)

    def owner(way, hop, sgn):
        hops = len(HOPS[way])
        return (z + (sgn if way == "L" else -sgn) * (hops + 1 - hop) + 16) % 8

    net.send("d_near", d_ref, dg.at[0, r], me.x_near())
    net.send("d_cross", d_ref, dg.at[2, r], me.x_cross())
    net.send("d_far", d_ref, dg.at[2, r], me.x_far())
    net.send("d_core", d_ref, dg.at[1, r], me.other_core())
    for o in (1, 3):
        net.send(("d", 0, o), d_ref, dg.at[0, r], me.at_y(-o))
    net.send("a_core", a_ref.at[xh, :, 1 - core], a4.at[0], me.other_core())
    for way, hop in A_ORDER:
        n = owner(way, hop, sign)
        net.send(("a_far", way, hop), a_ref.at[1 - xh, n, core], a4.at[1, n], me.x_far())
        n = owner(way, hop, -sign)
        net.send(("a_cross", way, hop), a_ref.at[1 - xh, n, 1 - core], a4.at[2, n], me.x_far_core())
    dg[0, r] = d_ref[...]
    for key, k, row in (("d_near", 0, near), ("d_cross", 2, near), ("d_far", 2, r)):
        net.wait(key)
        piece = dg.at[k, row]
        for o in (1, 3):
            net.send((key, o), piece, piece, me.at_y(-o))
        net.send((key, "core"), piece, dg.at[k + 1, row], me.other_core())

    def y_of(f):
        return (me.y + Y_ORDER[f]) % 4

    def commands_in(f):
        o = Y_ORDER[f]
        two = pl.ds(y_of(f) * 2, 2)
        if f == 0:
            for key in ("d_core", ("d_near", "core"), ("d_cross", "core"), ("d_far", "core"), "a_core"):
                net.wait(key)
            return
        if o == 2:
            net.wait("relay0")
            net.wait("relay2")
        else:
            for key in (("d", 0, o), ("d_near", o), ("d_cross", o), ("d_far", o)):
                net.wait(key)
        if o == 3:
            net.send("relay0", dg.at[0, two], dg.at[0, two], me.at_y(1))
        if o == 1:
            net.send("relay2", dg.at[2, two], dg.at[2, two], me.at_y(-1))
        for k in (0, 2):
            net.send(("core", k, o), dg.at[k, two], dg.at[k + 1, two], me.other_core())
        for k in (0, 2):
            net.wait(("core", k, o))

    arrived = set()

    def product(f, pieces):
        for piece in pieces:
            if piece not in arrived:
                arrived.add(piece)
                net.wait(("a_far",) + piece)
                net.wait(("a_cross",) + piece)
        owners = [owner(way, hop, sign) for way, hop in pieces]
        total = None
        for k in range(4):
            if k == 0:
                rows = [a_ref[xh, n, core] for n in owners]
            else:
                rows = [a4[k - 1, n] for n in owners]
            part = lax.dot_general(
                jnp.concatenate(rows, axis=0),
                dg[k, pl.ds(y_of(f) * 2, 2)].reshape(CHUNK, 256),
                (((1,), (1,)), ((), ())),
                preferred_element_type=F32,
            )
            total = part if total is None else total + part
        return [total[i * 64 : (i + 1) * 64] for i in range(len(pieces))]

    slots = {}
    for way, kinds in HOPS.items():
        for hop, kind in enumerate(kinds, 1):
            slots[way, hop] = (kind, sum(1 for k, _ in slots.values() if k is kind))

    def buffer(f, way, hop, sending):
        kind, n = slots[way, hop]
        if kind is BF:
            return (sb if sending else rb).at[f, n]
        return (sf if sending else rf).at[f, n]

    def stage(f, hop):
        if hop == 1:
            commands_in(f)
        pieces = [(way, hop) for way in HOPS if hop <= len(HOPS[way])]
        for (way, _), value in zip(pieces, product(f, pieces)):
            step = sign if way == "L" else -sign
            if hop > 1:
                net.wait((f, way, hop - 1))
                value += buffer(f, way, hop - 1, False)[...].astype(F32)
            out = buffer(f, way, hop, True)
            out[...] = value.astype(HOPS[way][hop - 1])
            net.send((f, way, hop), out, buffer(f, way, hop, False), me.at_z(step))

    def total(f):
        (value,) = product(f, [("L", 5)])
        for way in ("S", "L"):
            net.wait((f, way, len(HOPS[way])))
            value += buffer(f, way, len(HOPS[way]), False)[...].astype(F32)
        r_ref[:, pl.ds(pl.multiple_of(y_of(f) * CHUNK, CHUNK), CHUNK)] = value

    todo = [(f + (hop - 0.5 if hop > 1 else 0), f, hop) for f in range(CHUNKS) for hop in range(1, 6)]
    for _, f, hop in sorted(todo):
        if hop < 5:
            stage(f, hop)
        else:
            total(f)
    net.finish()


def gather_kernel(o_ref, osh_ref, rows_ref, cols_ref, send_sem, recv_sem):
    me = Place()
    r, c, z, xh = me.r, me.c, me.z, me.xh
    target = ((c + 4) % 8, r * 4 + c // 8)
    source = (c // 4, (c % 4) * 8 + (r + 4) % 8)
    greet(
        [me.other_core(), me.x_near(), me.x_far(), me.at_z(1), me.at_z(-1), me.at_y(1), me.at_y(-1)]
        + [target, source]
    )
    net = Net(send_sem, recv_sem)
    first, second = pl.ds(0, 32), pl.ds(32, 32)
    hops = {"L": 4, "S": 3}
    step = {"L": me.sign, "S": -me.sign}

    def slot(other, dz):
        return me.col((1 - xh) if other else xh, (z + dz + 16) % 8, me.core)

    def pass_on(key, n, half, device):
        piece = rows_ref.at[n, half]
        net.send(key, piece, piece, device)

    net.send("x1", o_ref.at[first], rows_ref.at[c, first], me.x_far())
    net.send("permute", osh_ref, cols_ref.at[c % 8], target)
    for way in hops:
        net.send(("z2", way, 1), o_ref.at[second], rows_ref.at[c, second], me.at_z(step[way]))
    for way in hops:
        net.send(("z1", way, 1), o_ref.at[first], rows_ref.at[c, first], me.at_z(step[way]))
    net.send(("x2", "own", 0), o_ref.at[second], rows_ref.at[c, second], me.x_far())
    net.send("core_own", o_ref, rows_ref.at[c], me.other_core())
    rows_ref[c] = o_ref[...]
    net.wait("x1")
    for way in hops:
        pass_on(("z1p", way, 1), slot(True, 0), first, me.at_z(step[way]))

    def to_core(key, n):
        net.send(key, rows_ref.at[n], rows_ref.at[n], me.other_core())

    def col_slot(row):
        return (row + 4) % 8

    def pass_col(key, row, device):
        piece = cols_ref.at[col_slot(row)]
        net.send(key, piece, piece, device)

    near = me.y * 2 + (1 - me.xl)
    for t in range(1, 5):
        ways = [way for way in hops if t <= hops[way]]
        for kind, half in (("z2", second), ("z1", first), ("z1p", first)):
            for way in ways:
                n = slot(kind == "z1p", -step[way] * t)
                net.wait((kind, way, t))
                if t < hops[way]:
                    pass_on((kind, way, t + 1), n, half, me.at_z(step[way]))
                if kind == "z2":
                    pass_on(("x2", way, t), n, second, me.x_far())
                if kind == "z1":
                    to_core(("core", way, t), n)
        if t == 1:
            net.wait("permute")
            pass_col("near", r, me.x_near())
            pass_col(("y0", 1), r, me.at_y(1))
            pass_col(("y0", -1), r, me.at_y(-1))
        if t == 2:
            net.wait("near")
            pass_col(("y1", 1), near, me.at_y(1))
            pass_col(("y1", -1), near, me.at_y(-1))
        if t == 3:
            net.wait(("y0", 1))
            pass_col(("y2", 1), (r + 6) % 8, me.at_y(1))
            net.wait(("y1", -1))
            pass_col(("y2", -1), (near + 2) % 8, me.at_y(-1))
    net.wait(("x2", "own", 0))
    to_core(("core_far", "own", 0), slot(True, 0))
    for t in range(1, 5):
        for way in hops:
            if t <= hops[way]:
                net.wait(("x2", way, t))
                to_core(("core_far", way, t), slot(True, -step[way] * t))
    for key in [("y0", -1), ("y1", 1), ("y2", 1), ("y2", -1), "core_own"]:
        net.wait(key)
    for key, entry in net.copies.items():
        if not entry[1]:
            net.wait(key)
    net.finish()


def reduced(interaction, commands):
    kinds = [kind for way in HOPS.values() for kind in way]
    n_bf, n_f32 = kinds.count(BF), kinds.count(F32)
    piece = (64, CHUNK)
    copies = 80
    return pl.pallas_call(
        reduce_kernel,
        out_shape=jax.ShapeDtypeStruct((64, FRAMES), F32),
        in_specs=[VMEM] * 2,
        out_specs=VMEM,
        scratch_shapes=[
            pltpu.VMEM((3, 8, 64, 256), BF),
            pltpu.VMEM((4, 8, 128, 256), BF),
            pltpu.VMEM((CHUNKS, n_bf) + piece, BF),
            pltpu.VMEM((CHUNKS, n_bf) + piece, BF),
            pltpu.VMEM((CHUNKS, n_f32) + piece, F32),
            pltpu.VMEM((CHUNKS, n_f32) + piece, F32),
            pltpu.SemaphoreType.DMA((copies,)),
            pltpu.SemaphoreType.DMA((copies,)),
        ],
        compiler_params=pltpu.CompilerParams(collective_id=0, has_side_effects=True),
        name="reduce_slopes",
    )(interaction.reshape(2, 8, 2, 64, 256), commands)


def gathered(openloop, shifted):
    return pl.pallas_call(
        gather_kernel,
        out_shape=(
            jax.ShapeDtypeStruct((32, 64, FRAMES), BF),
            jax.ShapeDtypeStruct((8, 64, FRAMES), BF),
        ),
        in_specs=[VMEM] * 2,
        out_specs=(VMEM, VMEM),
        scratch_shapes=[pltpu.SemaphoreType.DMA((80,)), pltpu.SemaphoreType.DMA((80,))],
        compiler_params=pltpu.CompilerParams(collective_id=1, has_side_effects=True),
        name="gather_slopes",
    )(openloop, shifted)


def delay_frames(response, frame_lag):
    margin = FRAMES // 4
    padded = jnp.concatenate(
        [jnp.zeros((response.shape[0], margin), response.dtype), response], axis=1
    )
    return lax.dynamic_slice_in_dim(padded, margin - frame_lag[0], FRAMES, 1)


def mask_frames(summed, frame_count):
    frame_index = lax.broadcasted_iota(jnp.int32, summed.shape, 1)
    return jnp.where(frame_index < frame_count[0], summed, 0.0).astype(BF)


def local(interaction, commands, slopes_measured, frame_lag, frame_count):
    response = reduced(interaction, commands)
    summed = delay_frames(response, frame_lag) + slopes_measured.astype(F32)
    openloop = mask_frames(summed, frame_count)
    shifted = jnp.concatenate([jnp.zeros((64, 1), BF), openloop[:, :-1]], axis=1)
    rows, cols = gathered(openloop, shifted)
    tile = lax.dot_general(
        rows.reshape(2048, FRAMES),
        cols.reshape(512, FRAMES),
        (((1,), (1,)), ((), ())),
        preferred_element_type=F32,
    )
    return tile * (1.0 / math.sqrt(FRAMES))


def solution(mesh):
    return jax.shard_map(
        local,
        mesh=mesh,
        in_specs=(P("rows", "cols"), P("rows", "cols"), P(("rows", "cols"), None), P(), P()),
        out_specs=P("rows", "cols"),
        check_vma=False,
    )
```

```python
import math

import jax
import jax.numpy as jnp
from jax import lax
from jax.experimental import pallas as pl
from jax.experimental.pallas import tpu as pltpu
from jax.sharding import PartitionSpec as P

FRAMES = 1024
CHUNK = 256
MARGIN = FRAMES // 4
CHUNKS = FRAMES // CHUNK
BF, F32 = jnp.bfloat16, jnp.float32
VMEM = pl.BlockSpec(memory_space=pltpu.VMEM)
Y_ORDER = (0, 1, 3, 2)
HOPS = {"L": (BF, BF, F32, F32), "S": (BF, BF, F32)}
A_ORDER = (("L", 1), ("S", 1), ("L", 2), ("S", 2), ("L", 3), ("S", 3), ("L", 4), ("L", 5))


class Place:
    def __init__(self):
        self.r = lax.axis_index("rows")
        self.c = lax.axis_index("cols")
        self.y, self.xl = self.r // 2, self.r % 2
        self.xh, self.z, self.core = self.c // 16, (self.c // 2) % 8, self.c % 2
        self.sign = 1 - 2 * self.core

    def col(self, xh, z, core):
        return xh * 16 + z * 2 + core

    def at_z(self, dz):
        return self.r, self.col(self.xh, (self.z + dz + 16) % 8, self.core)

    def at_y(self, dy):
        return (self.r + 2 * dy + 8) % 8, self.c

    def x_far(self):
        return self.r, (self.c + 16) % 32

    def permuted(self):
        return (self.c + 4) % 8, self.r * 4 + self.c // 8

    def permuted_from(self):
        return self.c // 4, (self.c % 4) * 8 + (self.r + 4) % 8

    def x_far_core(self):
        return self.r, self.col(1 - self.xh, self.z, 1 - self.core)

    def x_cross(self):
        return self.y * 2 + (1 - self.xl), (self.c + 16) % 32

    def x_near(self):
        return self.y * 2 + (1 - self.xl), self.c

    def other_core(self):
        return self.r, self.c + self.sign


class Net:
    def __init__(self, send_sem, recv_sem):
        self.send_sem, self.recv_sem = send_sem, recv_sem
        self.copies = {}

    def send(self, key, src, dst, device):
        n = len(self.copies)
        copy = pltpu.make_async_remote_copy(
            src_ref=src,
            dst_ref=dst,
            send_sem=self.send_sem.at[n],
            recv_sem=self.recv_sem.at[n],
            device_id=device,
            device_id_type=pl.DeviceIdType.MESH,
        )
        copy.start()
        self.copies[key] = [copy, False]

    def wait(self, key):
        entry = self.copies[key]
        assert not entry[1]
        entry[0].wait_recv()
        entry[1] = True

    def finish(self):
        for copy, received in self.copies.values():
            assert received
            copy.wait_send()


def greet(devices):
    barrier = pltpu.get_barrier_semaphore()
    for device in devices:
        pl.semaphore_signal(barrier, inc=1, device_id=device, device_id_type=pl.DeviceIdType.MESH)
    pl.semaphore_wait(barrier, len(devices))


def reduce_slopes(me, net, a_ref, d_ref, response, a4, dg, sb, rb, sf, rf):
    r, z, xh, core, sign = me.r, me.z, me.xh, me.core, me.sign
    near = me.y * 2 + (1 - me.xl)

    def owner(way, hop, sgn):
        hops = len(HOPS[way])
        return (z + (sgn if way == "L" else -sgn) * (hops + 1 - hop) + 16) % 8

    net.send("d_near", d_ref, dg.at[0, r], me.x_near())
    net.send("d_cross", d_ref, dg.at[2, r], me.x_cross())
    net.send("d_far", d_ref, dg.at[2, r], me.x_far())
    net.send("d_core", d_ref, dg.at[1, r], me.other_core())
    for o in (1, 3):
        net.send(("d", o), d_ref, dg.at[0, r], me.at_y(-o))
    net.send("a_core", a_ref.at[xh, :, 1 - core], a4.at[0], me.other_core())
    for way, hop in A_ORDER:
        n = owner(way, hop, sign)
        net.send(("a_far", way, hop), a_ref.at[1 - xh, n, core], a4.at[1, n], me.x_far())
        n = owner(way, hop, -sign)
        net.send(("a_cross", way, hop), a_ref.at[1 - xh, n, 1 - core], a4.at[2, n], me.x_far_core())
    dg[0, r] = d_ref[...]
    for key, k, row in (("d_near", 0, near), ("d_cross", 2, near), ("d_far", 2, r)):
        net.wait(key)
        piece = dg.at[k, row]
        for o in (1, 3):
            net.send((key, o), piece, piece, me.at_y(-o))
        net.send((key, "core"), piece, dg.at[k + 1, row], me.other_core())

    def y_of(f):
        return (me.y + Y_ORDER[f]) % 4

    def commands_in(f):
        o = Y_ORDER[f]
        two = pl.ds(y_of(f) * 2, 2)
        if f == 0:
            for key in ("d_core", ("d_near", "core"), ("d_cross", "core"), ("d_far", "core"), "a_core"):
                net.wait(key)
            return
        for key, k, side in (("d", 0, me.xl), ("d_near", 0, 1 - me.xl), ("d_cross", 2, 1 - me.xl), ("d_far", 2, me.xl)):
            if o == 2:
                net.wait(("relay", key))
                continue
            net.wait((key, o))
            piece = dg.at[k, y_of(f) * 2 + side]
            if (o, k) in ((3, 0), (1, 2)):
                net.send(("relay", key), piece, piece, me.at_y(1 if o == 3 else -1))
        for k in (0, 2):
            net.send(("core", k, o), dg.at[k, two], dg.at[k + 1, two], me.other_core())
        for k in (0, 2):
            net.wait(("core", k, o))

    arrived = set()

    def product(f, pieces):
        for piece in pieces:
            if piece not in arrived:
                arrived.add(piece)
                net.wait(("a_far",) + piece)
                net.wait(("a_cross",) + piece)
        owners = [owner(way, hop, sign) for way, hop in pieces]
        total = None
        for k in range(4):
            if k == 0:
                rows = [a_ref[xh, n, core] for n in owners]
            else:
                rows = [a4[k - 1, n] for n in owners]
            part = lax.dot_general(
                jnp.concatenate(rows, axis=0),
                dg[k, pl.ds(y_of(f) * 2, 2)].reshape(CHUNK, 256),
                (((1,), (1,)), ((), ())),
                preferred_element_type=F32,
            )
            total = part if total is None else total + part
        return [total[i * 64 : (i + 1) * 64] for i in range(len(pieces))]

    slots = {}
    for way, kinds in HOPS.items():
        for hop, kind in enumerate(kinds, 1):
            slots[way, hop] = (kind, sum(1 for k, _ in slots.values() if k is kind))

    def buffer(f, way, hop, sending):
        kind, n = slots[way, hop]
        if kind is BF:
            return (sb if sending else rb).at[f, n]
        return (sf if sending else rf).at[f, n]

    def stage(f, hop):
        if hop == 1:
            commands_in(f)
        pieces = [(way, hop) for way in HOPS if hop <= len(HOPS[way])]
        for (way, _), value in zip(pieces, product(f, pieces)):
            step = sign if way == "L" else -sign
            if hop > 1:
                net.wait((f, way, hop - 1))
                value += buffer(f, way, hop - 1, False)[...].astype(F32)
            out = buffer(f, way, hop, True)
            out[...] = value.astype(HOPS[way][hop - 1])
            net.send((f, way, hop), out, buffer(f, way, hop, False), me.at_z(step))

    def total(f):
        (value,) = product(f, [("L", 5)])
        for way in ("S", "L"):
            net.wait((f, way, len(HOPS[way])))
            value += buffer(f, way, len(HOPS[way]), False)[...].astype(F32)
        start = pl.multiple_of(MARGIN + y_of(f) * CHUNK, CHUNK)
        response[:, pl.ds(start, CHUNK)] = value

    todo = [(f + (hop - 0.5 if hop > 1 else 0), f, hop) for f in range(CHUNKS) for hop in range(1, 6)]
    for _, f, hop in sorted(todo):
        if hop < 5:
            stage(f, hop)
        else:
            total(f)


def open_loop(response, s_ref, lag_ref, count_ref, o_ref, osh_ref):
    window = response[...]
    lag = jnp.full(window.shape, lag_ref[0], jnp.int32)
    for bit in range(MARGIN.bit_length()):
        moved = pltpu.roll(window, 1 << bit, 1)
        window = jnp.where((lag & (1 << bit)) != 0, moved, window)
    summed = window[:, MARGIN:] + s_ref[...].astype(F32)
    frame = lax.broadcasted_iota(jnp.int32, summed.shape, 1)
    count = jnp.full(summed.shape, count_ref[0], jnp.int32)
    value = jnp.where(frame < count, summed, 0.0).astype(BF)
    o_ref[...] = value
    later = pltpu.roll(value.astype(F32), 1, 1)
    osh_ref[...] = jnp.where(frame == 0, 0.0, later).astype(BF)


def gather_slopes(me, net, o_ref, osh_ref, rows_ref, cols_ref):
    r, c, z, xh = me.r, me.c, me.z, me.xh
    target = me.permuted()
    first, second = pl.ds(0, 32), pl.ds(32, 32)
    hops = {"L": 4, "S": 3}
    step = {"L": me.sign, "S": -me.sign}

    def slot(other, dz):
        return me.col((1 - xh) if other else xh, (z + dz + 16) % 8, me.core)

    def pass_on(key, n, half, device):
        piece = rows_ref.at[n, half]
        net.send(key, piece, piece, device)

    net.send("x1", o_ref.at[first], rows_ref.at[c, first], me.x_far())
    net.send("permute", osh_ref, cols_ref.at[c % 8], target)
    for way in hops:
        net.send(("z2", way, 1), o_ref.at[second], rows_ref.at[c, second], me.at_z(step[way]))
    for way in hops:
        net.send(("z1", way, 1), o_ref.at[first], rows_ref.at[c, first], me.at_z(step[way]))
    net.send(("x2", "own", 0), o_ref.at[second], rows_ref.at[c, second], me.x_far())
    net.send("core_own", o_ref, rows_ref.at[c], me.other_core())
    rows_ref[c] = o_ref[...]
    net.wait("x1")
    for way in hops:
        pass_on(("z1p", way, 1), slot(True, 0), first, me.at_z(step[way]))

    def to_core(key, n):
        net.send(key, rows_ref.at[n], rows_ref.at[n], me.other_core())

    def col_slot(row):
        return (row + 4) % 8

    def pass_col(key, row, device):
        piece = cols_ref.at[col_slot(row)]
        net.send(key, piece, piece, device)

    near = me.y * 2 + (1 - me.xl)
    for t in range(1, 5):
        ways = [way for way in hops if t <= hops[way]]
        for kind, half in (("z2", second), ("z1", first), ("z1p", first)):
            for way in ways:
                n = slot(kind == "z1p", -step[way] * t)
                net.wait((kind, way, t))
                if t < hops[way]:
                    pass_on((kind, way, t + 1), n, half, me.at_z(step[way]))
                if kind == "z2":
                    pass_on(("x2", way, t), n, second, me.x_far())
                if kind == "z1":
                    to_core(("core", way, t), n)
        if t == 1:
            net.wait("permute")
            pass_col("near", r, me.x_near())
            pass_col(("y0", 1), r, me.at_y(1))
            pass_col(("y0", -1), r, me.at_y(-1))
        if t == 2:
            net.wait("near")
            pass_col(("y1", 1), near, me.at_y(1))
            pass_col(("y1", -1), near, me.at_y(-1))
        if t == 3:
            net.wait(("y0", 1))
            pass_col(("y2", 1), (r + 6) % 8, me.at_y(1))
            net.wait(("y1", -1))
            pass_col(("y2", -1), (near + 2) % 8, me.at_y(-1))
    net.wait(("x2", "own", 0))
    to_core(("core_far", "own", 0), slot(True, 0))
    for t in range(1, 5):
        for way in hops:
            if t <= hops[way]:
                net.wait(("x2", way, t))
                to_core(("core_far", way, t), slot(True, -step[way] * t))
    for key in [("y0", -1), ("y1", 1), ("y2", 1), ("y2", -1), "core_own"]:
        net.wait(key)
    for key, entry in net.copies.items():
        if not entry[1]:
            net.wait(key)


def kernel(
    a_ref, d_ref, s_ref, lag_ref, count_ref, rows_ref, cols_ref,
    response, o_scr, osh_scr, a4, dg, sb, rb, sf, rf, send_sem, recv_sem,
):
    me = Place()
    greet(
        [me.other_core(), me.x_near(), me.x_far(), me.x_cross(), me.x_far_core(), me.at_z(1), me.at_z(-1)]
        + [me.at_y(1), me.at_y(-1), me.permuted(), me.permuted_from()]
    )
    net = Net(send_sem, recv_sem)
    response[:, :MARGIN] = jnp.zeros((64, MARGIN), F32)
    reduce_slopes(me, net, a_ref, d_ref, response, a4, dg, sb, rb, sf, rf)
    open_loop(response, s_ref, lag_ref, count_ref, o_scr, osh_scr)
    gather_slopes(me, net, o_scr, osh_scr, rows_ref, cols_ref)
    net.finish()


def gathered(interaction, commands, slopes_measured, frame_lag, frame_count):
    kinds = [kind for way in HOPS.values() for kind in way]
    n_bf, n_f32 = kinds.count(BF), kinds.count(F32)
    piece = (64, CHUNK)
    copies = 160
    smem = pl.BlockSpec(memory_space=pltpu.SMEM)
    return pl.pallas_call(
        kernel,
        out_shape=(
            jax.ShapeDtypeStruct((32, 64, FRAMES), BF),
            jax.ShapeDtypeStruct((8, 64, FRAMES), BF),
        ),
        in_specs=[VMEM, VMEM, VMEM, smem, smem],
        out_specs=(VMEM, VMEM),
        scratch_shapes=[
            pltpu.VMEM((64, MARGIN + FRAMES), F32),
            pltpu.VMEM((64, FRAMES), BF),
            pltpu.VMEM((64, FRAMES), BF),
            pltpu.VMEM((3, 8, 64, 256), BF),
            pltpu.VMEM((4, 8, 128, 256), BF),
            pltpu.VMEM((CHUNKS, n_bf) + piece, BF),
            pltpu.VMEM((CHUNKS, n_bf) + piece, BF),
            pltpu.VMEM((CHUNKS, n_f32) + piece, F32),
            pltpu.VMEM((CHUNKS, n_f32) + piece, F32),
            pltpu.SemaphoreType.DMA((copies,)),
            pltpu.SemaphoreType.DMA((copies,)),
        ],
        compiler_params=pltpu.CompilerParams(
            collective_id=0, has_side_effects=True, vmem_limit_bytes=24 * 2**20
        ),
        name="open_loop_slopes",
    )(interaction.reshape(2, 8, 2, 64, 256), commands, slopes_measured, frame_lag, frame_count)


def local(interaction, commands, slopes_measured, frame_lag, frame_count):
    rows, cols = gathered(interaction, commands, slopes_measured, frame_lag, frame_count)
    tile = lax.dot_general(
        rows.reshape(2048, FRAMES),
        cols.reshape(512, FRAMES),
        (((1,), (1,)), ((), ())),
        preferred_element_type=F32,
    )
    return tile * (1.0 / math.sqrt(FRAMES))


def solution(mesh):
    return jax.shard_map(
        local,
        mesh=mesh,
        in_specs=(P("rows", "cols"), P("rows", "cols"), P(("rows", "cols"), None), P(), P()),
        out_specs=P("rows", "cols"),
        check_vma=False,
    )
```

```python
import math

import jax
import jax.numpy as jnp
from jax import lax
from jax.experimental import pallas as pl
from jax.experimental.pallas import tpu as pltpu
from jax.sharding import PartitionSpec as P

FRAMES = 1024
CHUNK = 256
MARGIN = FRAMES // 4
CHUNKS = FRAMES // CHUNK
BF, F32 = jnp.bfloat16, jnp.float32
VMEM = pl.BlockSpec(memory_space=pltpu.VMEM)
Y_ORDER = (0, 1, 3, 2)
HOPS = {"L": (BF, BF, F32, F32), "S": (BF, BF, F32)}
A_ORDER = (("L", 1), ("S", 1), ("L", 2), ("S", 2), ("L", 3), ("S", 3), ("L", 4), ("L", 5))


class Place:
    def __init__(self):
        self.r = lax.axis_index("rows")
        self.c = lax.axis_index("cols")
        self.y, self.xl = self.r // 2, self.r % 2
        self.xh, self.z, self.core = self.c // 16, (self.c // 2) % 8, self.c % 2
        self.sign = 1 - 2 * self.core

    def col(self, xh, z, core):
        return xh * 16 + z * 2 + core

    def at_z(self, dz):
        return self.r, self.col(self.xh, (self.z + dz + 16) % 8, self.core)

    def at_y(self, dy):
        return (self.r + 2 * dy + 8) % 8, self.c

    def x_far(self):
        return self.r, (self.c + 16) % 32

    def permuted(self):
        return (self.c + 4) % 8, self.r * 4 + self.c // 8

    def permuted_from(self):
        return self.c // 4, (self.c % 4) * 8 + (self.r + 4) % 8

    def x_far_core(self):
        return self.r, self.col(1 - self.xh, self.z, 1 - self.core)

    def x_cross(self):
        return self.y * 2 + (1 - self.xl), (self.c + 16) % 32

    def x_near(self):
        return self.y * 2 + (1 - self.xl), self.c

    def other_core(self):
        return self.r, self.c + self.sign


class Net:
    def __init__(self, send_sem, recv_sem):
        self.send_sem, self.recv_sem = send_sem, recv_sem
        self.copies = {}

    def send(self, key, src, dst, device):
        n = len(self.copies)
        copy = pltpu.make_async_remote_copy(
            src_ref=src,
            dst_ref=dst,
            send_sem=self.send_sem.at[n],
            recv_sem=self.recv_sem.at[n],
            device_id=device,
            device_id_type=pl.DeviceIdType.MESH,
        )
        copy.start()
        self.copies[key] = [copy, False]

    def wait(self, key):
        entry = self.copies[key]
        assert not entry[1]
        entry[0].wait_recv()
        entry[1] = True

    def finish(self):
        for copy, received in self.copies.values():
            assert received
            copy.wait_send()


def greet(devices):
    barrier = pltpu.get_barrier_semaphore()
    for device in devices:
        pl.semaphore_signal(barrier, inc=1, device_id=device, device_id_type=pl.DeviceIdType.MESH)
    pl.semaphore_wait(barrier, len(devices))


def reduce_slopes(me, net, a_ref, d_ref, response, a4, dg, sb, rb, sf, rf):
    r, z, xh, core, sign = me.r, me.z, me.xh, me.core, me.sign
    near = me.y * 2 + (1 - me.xl)

    def owner(way, hop, sgn):
        hops = len(HOPS[way])
        return (z + (sgn if way == "L" else -sgn) * (hops + 1 - hop) + 16) % 8

    net.send("d_near", d_ref, dg.at[0, r], me.x_near())
    net.send("d_cross", d_ref, dg.at[2, r], me.x_cross())
    net.send("d_far", d_ref, dg.at[2, r], me.x_far())
    net.send("d_core", d_ref, dg.at[1, r], me.other_core())
    for o in (1, 3):
        net.send(("d", o), d_ref, dg.at[0, r], me.at_y(-o))
    net.send("a_core", a_ref.at[xh, :, 1 - core], a4.at[0], me.other_core())
    for way, hop in A_ORDER:
        n = owner(way, hop, sign)
        net.send(("a_far", way, hop), a_ref.at[1 - xh, n, core], a4.at[1, n], me.x_far())
        n = owner(way, hop, -sign)
        net.send(("a_cross", way, hop), a_ref.at[1 - xh, n, 1 - core], a4.at[2, n], me.x_far_core())
    dg[0, r] = d_ref[...]
    for key, k, row in (("d_near", 0, near), ("d_cross", 2, near), ("d_far", 2, r)):
        net.wait(key)
        piece = dg.at[k, row]
        for o in (1, 3):
            net.send((key, o), piece, piece, me.at_y(-o))
        net.send((key, "core"), piece, dg.at[k + 1, row], me.other_core())

    def y_of(f):
        return (me.y + Y_ORDER[f]) % 4

    def commands_in(f):
        o = Y_ORDER[f]
        two = pl.ds(y_of(f) * 2, 2)
        if f == 0:
            for key in ("d_core", ("d_near", "core"), ("d_cross", "core"), ("d_far", "core"), "a_core"):
                net.wait(key)
            return
        for key, k, side in (("d", 0, me.xl), ("d_near", 0, 1 - me.xl), ("d_cross", 2, 1 - me.xl), ("d_far", 2, me.xl)):
            if o == 2:
                net.wait(("relay", key))
                continue
            net.wait((key, o))
            piece = dg.at[k, y_of(f) * 2 + side]
            if (o, k) in ((3, 0), (1, 2)):
                net.send(("relay", key), piece, piece, me.at_y(1 if o == 3 else -1))
        for k in (0, 2):
            net.send(("core", k, o), dg.at[k, two], dg.at[k + 1, two], me.other_core())
        for k in (0, 2):
            net.wait(("core", k, o))

    arrived = set()

    def product(f, pieces):
        for piece in pieces:
            if piece not in arrived:
                arrived.add(piece)
                net.wait(("a_far",) + piece)
                net.wait(("a_cross",) + piece)
        owners = [owner(way, hop, sign) for way, hop in pieces]
        total = None
        for k in range(4):
            if k == 0:
                rows = [a_ref[xh, n, core] for n in owners]
            else:
                rows = [a4[k - 1, n] for n in owners]
            part = lax.dot_general(
                jnp.concatenate(rows, axis=0),
                dg[k, pl.ds(y_of(f) * 2, 2)].reshape(CHUNK, 256),
                (((1,), (1,)), ((), ())),
                preferred_element_type=F32,
            )
            total = part if total is None else total + part
        return [total[i * 64 : (i + 1) * 64] for i in range(len(pieces))]

    slots = {}
    for way, kinds in HOPS.items():
        for hop, kind in enumerate(kinds, 1):
            slots[way, hop] = (kind, sum(1 for k, _ in slots.values() if k is kind))

    def buffer(f, way, hop, sending):
        kind, n = slots[way, hop]
        if kind is BF:
            return (sb if sending else rb).at[f, n]
        return (sf if sending else rf).at[f, n]

    def stage(f, hop):
        if hop == 1:
            commands_in(f)
        pieces = [(way, hop) for way in HOPS if hop <= len(HOPS[way])]
        for (way, _), value in zip(pieces, product(f, pieces)):
            step = sign if way == "L" else -sign
            if hop > 1:
                net.wait((f, way, hop - 1))
                value += buffer(f, way, hop - 1, False)[...].astype(F32)
            out = buffer(f, way, hop, True)
            out[...] = value.astype(HOPS[way][hop - 1])
            net.send((f, way, hop), out, buffer(f, way, hop, False), me.at_z(step))

    def total(f):
        (value,) = product(f, [("L", 5)])
        for way in ("S", "L"):
            net.wait((f, way, len(HOPS[way])))
            value += buffer(f, way, len(HOPS[way]), False)[...].astype(F32)
        start = pl.multiple_of(MARGIN + y_of(f) * CHUNK, CHUNK)
        response[:, pl.ds(start, CHUNK)] = value

    todo = [(f + (hop - 0.5 if hop > 1 else 0), f, hop) for f in range(CHUNKS) for hop in range(1, 6)]
    for _, f, hop in sorted(todo):
        if hop < 5:
            stage(f, hop)
        else:
            total(f)


def open_loop(response, s_ref, lag_ref, count_ref, o_ref, osh_ref):
    window = response[...]
    lag = jnp.full(window.shape, lag_ref[0], jnp.int32)
    for bit in range(MARGIN.bit_length()):
        moved = pltpu.roll(window, 1 << bit, 1)
        window = jnp.where((lag & (1 << bit)) != 0, moved, window)
    summed = window[:, MARGIN:] + s_ref[...].astype(F32)
    frame = lax.broadcasted_iota(jnp.int32, summed.shape, 1)
    count = jnp.full(summed.shape, count_ref[0], jnp.int32)
    value = jnp.where(frame < count, summed, 0.0).astype(BF)
    o_ref[...] = value
    later = pltpu.roll(value.astype(F32), 1, 1)
    osh_ref[...] = jnp.where(frame == 0, 0.0, later).astype(BF)


def gather_slopes(me, net, o_ref, osh_ref, rows_ref, cols_ref):
    r, c, z, xh = me.r, me.c, me.z, me.xh
    target = me.permuted()
    first, second = pl.ds(0, 32), pl.ds(32, 32)
    hops = {"L": 4, "S": 3}
    step = {"L": me.sign, "S": -me.sign}

    def slot(other, dz):
        return me.col((1 - xh) if other else xh, (z + dz + 16) % 8, me.core)

    def pass_on(key, n, half, device):
        piece = rows_ref.at[n, half]
        net.send(key, piece, piece, device)

    near = me.y * 2 + (1 - me.xl)
    halves = (first, second)

    def to_core(key, n):
        net.send(key, rows_ref.at[n], rows_ref.at[n], me.other_core())

    def pass_col(key, row, half, device):
        piece = cols_ref.at[(row + 4) % 8, half]
        net.send(key, piece, piece, device)

    net.send("x1", o_ref.at[first], rows_ref.at[c, first], me.x_far())
    for p, half in enumerate(halves):
        net.send(("permute", p), osh_ref.at[half], cols_ref.at[c % 8, half], target)
    for way in hops:
        net.send(("z2", way, 1), o_ref.at[second], rows_ref.at[c, second], me.at_z(step[way]))
    for way in hops:
        net.send(("z1", way, 1), o_ref.at[first], rows_ref.at[c, first], me.at_z(step[way]))
    net.send(("x2", "own", 0), o_ref.at[second], rows_ref.at[c, second], me.x_far())
    net.send("core_own", o_ref, rows_ref.at[c], me.other_core())
    rows_ref[c] = o_ref[...]

    events = []

    def on(time, key, act=None):
        events.append((time, len(events), key, act))

    def relay(kind, half, way, t):
        def act():
            n = slot(kind == "z1p", -step[way] * t)
            if t < hops[way]:
                pass_on((kind, way, t + 1), n, half, me.at_z(step[way]))
            if kind == "z2":
                pass_on(("x2", way, t), n, second, me.x_far())
            if kind == "z1":
                to_core(("core", way, t), n)

        return act

    def cross_over():
        for way in hops:
            pass_on(("z1p", way, 1), slot(True, 0), first, me.at_z(step[way]))

    def far(way, t):
        n = slot(True, 0 if t == 0 else -step[way] * t)
        return lambda: to_core(("core_far", way, t), n)

    on(4, "x1", cross_over)
    on(12, ("x2", "own", 0), far("own", 0))
    for t in range(1, 5):
        for way in hops:
            if t <= hops[way]:
                on(4 * t, ("z2", way, t), relay("z2", second, way, t))
                on(4 * t + 1, ("z1", way, t), relay("z1", first, way, t))
                on(4 * t + 4.5, ("z1p", way, t), relay("z1p", first, way, t))
                on(4 * t + 7, ("x2", way, t), far(way, t))
    for p, half in enumerate(halves):
        def spread(p=p, half=half):
            pass_col(("near", p), r, half, me.x_near())
            for d in (1, -1):
                pass_col(("y0", p, d), r, half, me.at_y(d))

        def spread_near(p=p, half=half):
            for d in (1, -1):
                pass_col(("y1", p, d), near, half, me.at_y(d))

        late = 2 * p
        on(9 + late, ("permute", p), spread)
        on(13 + late, ("near", p), spread_near)
        on(14 + late, ("y0", p, 1), lambda p=p, half=half: pass_col(("y2", p, 1), (r + 6) % 8, half, me.at_y(1)))
        on(18 + late, ("y1", p, -1), lambda p=p, half=half: pass_col(("y2", p, -1), (near + 2) % 8, half, me.at_y(-1)))
    for _, _, key, act in sorted(events, key=lambda e: e[:2]):
        net.wait(key)
        if act is not None:
            act()
    for key, entry in net.copies.items():
        if not entry[1]:
            net.wait(key)


def kernel(
    a_ref, d_ref, s_ref, lag_ref, count_ref, rows_ref, cols_ref,
    response, o_scr, osh_scr, a4, dg, sb, rb, sf, rf, send_sem, recv_sem,
):
    me = Place()
    greet(
        [me.other_core(), me.x_near(), me.x_far(), me.x_cross(), me.x_far_core(), me.at_z(1), me.at_z(-1)]
        + [me.at_y(1), me.at_y(-1), me.permuted(), me.permuted_from()]
    )
    net = Net(send_sem, recv_sem)
    response[:, :MARGIN] = jnp.zeros((64, MARGIN), F32)
    reduce_slopes(me, net, a_ref, d_ref, response, a4, dg, sb, rb, sf, rf)
    open_loop(response, s_ref, lag_ref, count_ref, o_scr, osh_scr)
    gather_slopes(me, net, o_scr, osh_scr, rows_ref, cols_ref)
    net.finish()


def gathered(interaction, commands, slopes_measured, frame_lag, frame_count):
    kinds = [kind for way in HOPS.values() for kind in way]
    n_bf, n_f32 = kinds.count(BF), kinds.count(F32)
    piece = (64, CHUNK)
    copies = 160
    smem = pl.BlockSpec(memory_space=pltpu.SMEM)
    return pl.pallas_call(
        kernel,
        out_shape=(
            jax.ShapeDtypeStruct((32, 64, FRAMES), BF),
            jax.ShapeDtypeStruct((8, 64, FRAMES), BF),
        ),
        in_specs=[VMEM, VMEM, VMEM, smem, smem],
        out_specs=(VMEM, VMEM),
        scratch_shapes=[
            pltpu.VMEM((64, MARGIN + FRAMES), F32),
            pltpu.VMEM((64, FRAMES), BF),
            pltpu.VMEM((64, FRAMES), BF),
            pltpu.VMEM((3, 8, 64, 256), BF),
            pltpu.VMEM((4, 8, 128, 256), BF),
            pltpu.VMEM((CHUNKS, n_bf) + piece, BF),
            pltpu.VMEM((CHUNKS, n_bf) + piece, BF),
            pltpu.VMEM((CHUNKS, n_f32) + piece, F32),
            pltpu.VMEM((CHUNKS, n_f32) + piece, F32),
            pltpu.SemaphoreType.DMA((copies,)),
            pltpu.SemaphoreType.DMA((copies,)),
        ],
        compiler_params=pltpu.CompilerParams(
            collective_id=0, has_side_effects=True, vmem_limit_bytes=24 * 2**20
        ),
        name="open_loop_slopes",
    )(interaction.reshape(2, 8, 2, 64, 256), commands, slopes_measured, frame_lag, frame_count)


def local(interaction, commands, slopes_measured, frame_lag, frame_count):
    rows, cols = gathered(interaction, commands, slopes_measured, frame_lag, frame_count)
    tile = lax.dot_general(
        rows.reshape(2048, FRAMES),
        cols.reshape(512, FRAMES),
        (((1,), (1,)), ((), ())),
        preferred_element_type=F32,
    )
    return tile * (1.0 / math.sqrt(FRAMES))


def solution(mesh):
    return jax.shard_map(
        local,
        mesh=mesh,
        in_specs=(P("rows", "cols"), P("rows", "cols"), P(("rows", "cols"), None), P(), P()),
        out_specs=P("rows", "cols"),
        check_vma=False,
    )
```

```python
import math

import jax
import jax.numpy as jnp
from jax import lax
from jax.experimental import pallas as pl
from jax.experimental.pallas import tpu as pltpu
from jax.sharding import PartitionSpec as P

FRAMES = 1024
CHUNK = 256
MARGIN = FRAMES // 4
CHUNKS = FRAMES // CHUNK
BF, F32 = jnp.bfloat16, jnp.float32
VMEM = pl.BlockSpec(memory_space=pltpu.VMEM)
Y_ORDER = (0, 1, 3, 2)
HOPS = {"L": (BF, BF, F32, F32), "S": (BF, BF, F32)}
A_ORDER = (("L", 1), ("S", 1), ("L", 2), ("S", 2), ("L", 3), ("S", 3), ("L", 4), ("L", 5))


CHUNK_START = (8.5, 12.5, 12.6, 17.0)
HOP_TIME = 4.0
COL_LATE = -5.0


class Place:
    def __init__(self):
        self.r = lax.axis_index("rows")
        self.c = lax.axis_index("cols")
        self.y, self.xl = self.r // 2, self.r % 2
        self.xh, self.z, self.core = self.c // 16, (self.c // 2) % 8, self.c % 2
        self.sign = 1 - 2 * self.core

    def col(self, xh, z, core):
        return xh * 16 + z * 2 + core

    def at_z(self, dz):
        return self.r, self.col(self.xh, (self.z + dz + 16) % 8, self.core)

    def at_y(self, dy):
        return (self.r + 2 * dy + 8) % 8, self.c

    def x_far(self):
        return self.r, (self.c + 16) % 32

    def permuted(self):
        return (self.c + 4) % 8, self.r * 4 + self.c // 8

    def permuted_from(self):
        return self.c // 4, (self.c % 4) * 8 + (self.r + 4) % 8

    def x_far_core(self):
        return self.r, self.col(1 - self.xh, self.z, 1 - self.core)

    def x_cross(self):
        return self.y * 2 + (1 - self.xl), (self.c + 16) % 32

    def x_near(self):
        return self.y * 2 + (1 - self.xl), self.c

    def other_core(self):
        return self.r, self.c + self.sign


class Net:
    def __init__(self, send_sem, recv_sem):
        self.send_sem, self.recv_sem = send_sem, recv_sem
        self.copies = {}

    def send(self, key, src, dst, device):
        n = len(self.copies)
        copy = pltpu.make_async_remote_copy(
            src_ref=src,
            dst_ref=dst,
            send_sem=self.send_sem.at[n],
            recv_sem=self.recv_sem.at[n],
            device_id=device,
            device_id_type=pl.DeviceIdType.MESH,
        )
        copy.start()
        self.copies[key] = [copy, False]

    def wait(self, key):
        entry = self.copies[key]
        assert not entry[1]
        entry[0].wait_recv()
        entry[1] = True

    def finish(self):
        for copy, received in self.copies.values():
            assert received
            copy.wait_send()


def greet(devices):
    barrier = pltpu.get_barrier_semaphore()
    for device in devices:
        pl.semaphore_signal(barrier, inc=1, device_id=device, device_id_type=pl.DeviceIdType.MESH)
    pl.semaphore_wait(barrier, len(devices))


def reduce_slopes(me, net, a_ref, d_ref, response, a4, dg, sb, rb, sf, rf):
    r, z, xh, core, sign = me.r, me.z, me.xh, me.core, me.sign
    near = me.y * 2 + (1 - me.xl)

    def owner(way, hop, sgn):
        hops = len(HOPS[way])
        return (z + (sgn if way == "L" else -sgn) * (hops + 1 - hop) + 16) % 8

    net.send("d_far", d_ref, dg.at[2, r], me.x_far())
    net.send("d_near", d_ref, dg.at[0, r], me.x_near())
    net.send("d_cross", d_ref, dg.at[2, r], me.x_cross())
    net.send(("core", "d", 0), d_ref, dg.at[1, r], me.other_core())
    for o in (1, 3):
        net.send(("d", o), d_ref, dg.at[0, r], me.at_y(-o))
    net.send("a_core", a_ref.at[xh, :, 1 - core], a4.at[0], me.other_core())
    for way, hop in A_ORDER:
        n = owner(way, hop, sign)
        net.send(("a_far", way, hop), a_ref.at[1 - xh, n, core], a4.at[1, n], me.x_far())
        n = owner(way, hop, -sign)
        net.send(("a_cross", way, hop), a_ref.at[1 - xh, n, 1 - core], a4.at[2, n], me.x_far_core())
    dg[0, r] = d_ref[...]
    def y_of(f):
        return (me.y + Y_ORDER[f]) % 4

    pieces_of = (("d", 0, me.xl), ("d_near", 0, 1 - me.xl), ("d_cross", 2, 1 - me.xl), ("d_far", 2, me.xl))

    def from_x(key, k, row):
        def act():
            net.wait(key)
            piece = dg.at[k, row]
            for o in (1, 3):
                net.send((key, o), piece, piece, me.at_y(-o))
            net.send(("core", key, 0), piece, dg.at[k + 1, row], me.other_core())

        return act

    def from_y(key, k, side, o):
        def act():
            net.wait((key, o))
            row = (me.y + o) % 4 * 2 + side
            piece = dg.at[k, row]
            if (o, k) in ((3, 0), (1, 2)):
                net.send((key, 2), piece, piece, me.at_y(1 if o == 3 else -1))
            net.send(("core", key, o), piece, dg.at[k + 1, row], me.other_core())

        return act

    def commands_in(f):
        for key, _, _ in pieces_of:
            net.wait(("core", key, Y_ORDER[f]))
        if f == 0:
            net.wait("a_core")

    arrived = set()

    def product(f, pieces):
        for piece in pieces:
            if piece not in arrived:
                arrived.add(piece)
                net.wait(("a_far",) + piece)
                net.wait(("a_cross",) + piece)
        owners = [owner(way, hop, sign) for way, hop in pieces]
        total = None
        for k in range(4):
            if k == 0:
                rows = [a_ref[xh, n, core] for n in owners]
            else:
                rows = [a4[k - 1, n] for n in owners]
            part = lax.dot_general(
                jnp.concatenate(rows, axis=0),
                dg[k, pl.ds(y_of(f) * 2, 2)].reshape(CHUNK, 256),
                (((1,), (1,)), ((), ())),
                preferred_element_type=F32,
            )
            total = part if total is None else total + part
        return [total[i * 64 : (i + 1) * 64] for i in range(len(pieces))]

    slots = {}
    for way, kinds in HOPS.items():
        for hop, kind in enumerate(kinds, 1):
            slots[way, hop] = (kind, sum(1 for k, _ in slots.values() if k is kind))

    def buffer(f, way, hop, sending):
        kind, n = slots[way, hop]
        if kind is BF:
            return (sb if sending else rb).at[f, n]
        return (sf if sending else rf).at[f, n]

    def stage(f, hop):
        if hop == 1:
            commands_in(f)
        pieces = [(way, hop) for way in HOPS if hop <= len(HOPS[way])]
        for (way, _), value in zip(pieces, product(f, pieces)):
            step = sign if way == "L" else -sign
            if hop > 1:
                net.wait((f, way, hop - 1))
                value += buffer(f, way, hop - 1, False)[...].astype(F32)
            out = buffer(f, way, hop, True)
            out[...] = value.astype(HOPS[way][hop - 1])
            net.send((f, way, hop), out, buffer(f, way, hop, False), me.at_z(step))

    def total(f):
        (value,) = product(f, [("L", 5)])
        for way in ("S", "L"):
            net.wait((f, way, len(HOPS[way])))
            value += buffer(f, way, len(HOPS[way]), False)[...].astype(F32)
        start = pl.multiple_of(MARGIN + y_of(f) * CHUNK, CHUNK)
        response[:, pl.ds(start, CHUNK)] = value

    events = []

    def on(time, act):
        events.append((time, len(events), act))

    on(4.0, from_x("d_near", 0, near))
    on(4.2, from_x("d_cross", 2, near))
    on(6.0, from_x("d_far", 2, r))
    for o in (1, 3):
        for time, (key, k, side) in zip((4.5, 8.2, 9.0, 11.0), pieces_of):
            on(time, from_y(key, k, side, o))
    for time, (key, k, side) in zip((8.4, 12.0, 13.0, 15.0), pieces_of):
        on(time, from_y(key, k, side, 2))
    for f, begin in enumerate(CHUNK_START):
        for hop in range(1, 5):
            on(begin + HOP_TIME * (hop - 1), lambda f=f, hop=hop: stage(f, hop))
        on(begin + HOP_TIME * 4, lambda f=f: total(f))
    for _, _, act in sorted(events, key=lambda e: e[:2]):
        act()


def open_loop(response, s_ref, lag_ref, count_ref, o_ref, osh_ref):
    window = response[...]
    lag = jnp.full(window.shape, lag_ref[0], jnp.int32)
    for bit in range(MARGIN.bit_length()):
        moved = pltpu.roll(window, 1 << bit, 1)
        window = jnp.where((lag & (1 << bit)) != 0, moved, window)
    summed = window[:, MARGIN:] + s_ref[...].astype(F32)
    frame = lax.broadcasted_iota(jnp.int32, summed.shape, 1)
    count = jnp.full(summed.shape, count_ref[0], jnp.int32)
    value = jnp.where(frame < count, summed, 0.0).astype(BF)
    o_ref[...] = value
    later = pltpu.roll(value.astype(F32), 1, 1)
    osh_ref[...] = jnp.where(frame == 0, 0.0, later).astype(BF)


def gather_slopes(me, net, o_ref, osh_ref, rows_ref, cols_ref):
    r, c, z, xh = me.r, me.c, me.z, me.xh
    target = me.permuted()
    first, second = pl.ds(0, 32), pl.ds(32, 32)
    hops = {"L": 4, "S": 3}
    step = {"L": me.sign, "S": -me.sign}

    def slot(other, dz):
        return me.col((1 - xh) if other else xh, (z + dz + 16) % 8, me.core)

    def pass_on(key, n, half, device):
        piece = rows_ref.at[n, half]
        net.send(key, piece, piece, device)

    near = me.y * 2 + (1 - me.xl)
    halves = (first, second)

    def to_core(key, n):
        net.send(key, rows_ref.at[n], rows_ref.at[n], me.other_core())

    def pass_col(key, row, half, device):
        piece = cols_ref.at[(row + 4) % 8, half]
        net.send(key, piece, piece, device)

    net.send("x1", o_ref.at[first], rows_ref.at[c, first], me.x_far())
    for p, half in enumerate(halves):
        net.send(("permute", p), osh_ref.at[half], cols_ref.at[c % 8, half], target)
    for way in hops:
        net.send(("z2", way, 1), o_ref.at[second], rows_ref.at[c, second], me.at_z(step[way]))
    for way in hops:
        net.send(("z1", way, 1), o_ref.at[first], rows_ref.at[c, first], me.at_z(step[way]))
    net.send(("x2", "own", 0), o_ref.at[second], rows_ref.at[c, second], me.x_far())
    net.send("core_own", o_ref, rows_ref.at[c], me.other_core())
    rows_ref[c] = o_ref[...]

    events = []

    def on(time, key, act=None):
        events.append((time, len(events), key, act))

    def relay(kind, half, way, t):
        def act():
            n = slot(kind == "z1p", -step[way] * t)
            if t < hops[way]:
                pass_on((kind, way, t + 1), n, half, me.at_z(step[way]))
            if kind == "z2":
                pass_on(("x2", way, t), n, second, me.x_far())
            if kind == "z1":
                to_core(("core", way, t), n)

        return act

    def cross_over():
        for way in hops:
            pass_on(("z1p", way, 1), slot(True, 0), first, me.at_z(step[way]))

    def far(way, t):
        n = slot(True, 0 if t == 0 else -step[way] * t)
        return lambda: to_core(("core_far", way, t), n)

    on(4, "x1", cross_over)
    on(12, ("x2", "own", 0), far("own", 0))
    for t in range(1, 5):
        for way in hops:
            if t <= hops[way]:
                on(4 * t, ("z2", way, t), relay("z2", second, way, t))
                on(4 * t + 1, ("z1", way, t), relay("z1", first, way, t))
                on(4 * t + 4.5, ("z1p", way, t), relay("z1p", first, way, t))
                on(4 * t + 7, ("x2", way, t), far(way, t))
    for p, half in enumerate(halves):
        def spread(p=p, half=half):
            pass_col(("near", p), r, half, me.x_near())
            for d in (1, -1):
                pass_col(("y0", p, d), r, half, me.at_y(d))

        def spread_near(p=p, half=half):
            for d in (1, -1):
                pass_col(("y1", p, d), near, half, me.at_y(d))

        late = 2 * p + COL_LATE
        on(9 + late, ("permute", p), spread)
        on(13 + late, ("near", p), spread_near)
        on(14 + late, ("y0", p, 1), lambda p=p, half=half: pass_col(("y2", p, 1), (r + 6) % 8, half, me.at_y(1)))
        on(18 + late, ("y1", p, -1), lambda p=p, half=half: pass_col(("y2", p, -1), (near + 2) % 8, half, me.at_y(-1)))
    for _, _, key, act in sorted(events, key=lambda e: e[:2]):
        net.wait(key)
        if act is not None:
            act()
    for key, entry in net.copies.items():
        if not entry[1]:
            net.wait(key)


def kernel(
    a_ref, d_ref, s_ref, lag_ref, count_ref, rows_ref, cols_ref,
    response, o_scr, osh_scr, a4, dg, sb, rb, sf, rf, send_sem, recv_sem,
):
    me = Place()
    greet(
        [me.other_core(), me.x_near(), me.x_far(), me.x_cross(), me.x_far_core(), me.at_z(1), me.at_z(-1)]
        + [me.at_y(1), me.at_y(-1), me.permuted(), me.permuted_from()]
    )
    net = Net(send_sem, recv_sem)
    response[:, :MARGIN] = jnp.zeros((64, MARGIN), F32)
    reduce_slopes(me, net, a_ref, d_ref, response, a4, dg, sb, rb, sf, rf)
    open_loop(response, s_ref, lag_ref, count_ref, o_scr, osh_scr)
    gather_slopes(me, net, o_scr, osh_scr, rows_ref, cols_ref)
    net.finish()


def gathered(interaction, commands, slopes_measured, frame_lag, frame_count):
    kinds = [kind for way in HOPS.values() for kind in way]
    n_bf, n_f32 = kinds.count(BF), kinds.count(F32)
    piece = (64, CHUNK)
    copies = 160
    smem = pl.BlockSpec(memory_space=pltpu.SMEM)
    return pl.pallas_call(
        kernel,
        out_shape=(
            jax.ShapeDtypeStruct((32, 64, FRAMES), BF),
            jax.ShapeDtypeStruct((8, 64, FRAMES), BF),
        ),
        in_specs=[VMEM, VMEM, VMEM, smem, smem],
        out_specs=(VMEM, VMEM),
        scratch_shapes=[
            pltpu.VMEM((64, MARGIN + FRAMES), F32),
            pltpu.VMEM((64, FRAMES), BF),
            pltpu.VMEM((64, FRAMES), BF),
            pltpu.VMEM((3, 8, 64, 256), BF),
            pltpu.VMEM((4, 8, 128, 256), BF),
            pltpu.VMEM((CHUNKS, n_bf) + piece, BF),
            pltpu.VMEM((CHUNKS, n_bf) + piece, BF),
            pltpu.VMEM((CHUNKS, n_f32) + piece, F32),
            pltpu.VMEM((CHUNKS, n_f32) + piece, F32),
            pltpu.SemaphoreType.DMA((copies,)),
            pltpu.SemaphoreType.DMA((copies,)),
        ],
        compiler_params=pltpu.CompilerParams(
            collective_id=0, has_side_effects=True, vmem_limit_bytes=24 * 2**20
        ),
        name="open_loop_slopes",
    )(interaction.reshape(2, 8, 2, 64, 256), commands, slopes_measured, frame_lag, frame_count)


def local(interaction, commands, slopes_measured, frame_lag, frame_count):
    rows, cols = gathered(interaction, commands, slopes_measured, frame_lag, frame_count)
    tile = lax.dot_general(
        rows.reshape(2048, FRAMES),
        cols.reshape(512, FRAMES),
        (((1,), (1,)), ((), ())),
        preferred_element_type=F32,
    )
    return tile * (1.0 / math.sqrt(FRAMES))


def solution(mesh):
    return jax.shard_map(
        local,
        mesh=mesh,
        in_specs=(P("rows", "cols"), P("rows", "cols"), P(("rows", "cols"), None), P(), P()),
        out_specs=P("rows", "cols"),
        check_vma=False,
    )
```

```python
import functools
import math

import jax
import jax.numpy as jnp
from jax import lax
from jax.experimental import pallas as pl
from jax.experimental.pallas import tpu as pltpu
from jax.sharding import PartitionSpec as P

FRAMES = 1024
CHUNK = 256
BOUNDS = (512, 768, 1024)
MARGIN = FRAMES // 4
CHUNKS = FRAMES // CHUNK
BF, F32 = jnp.bfloat16, jnp.float32
VMEM = pl.BlockSpec(memory_space=pltpu.VMEM)
Y_ORDER = (0, 1, 3, 2)
HOPS = {"L": (BF, BF, F32, F32), "S": (BF, BF, F32)}
A_ORDER = (("L", 1), ("S", 1), ("L", 2), ("S", 2), ("L", 3), ("S", 3), ("L", 4), ("L", 5))


CHUNK_START = (8.5, 12.5, 12.6, 17.0)
HOP_TIME = 4.0
COL_LATE = -5.0


class Place:
    def __init__(self):
        self.r = lax.axis_index("rows")
        self.c = lax.axis_index("cols")
        self.y, self.xl = self.r // 2, self.r % 2
        self.xh, self.z, self.core = self.c // 16, (self.c // 2) % 8, self.c % 2
        self.sign = 1 - 2 * self.core

    def col(self, xh, z, core):
        return xh * 16 + z * 2 + core

    def at_z(self, dz):
        return self.r, self.col(self.xh, (self.z + dz + 16) % 8, self.core)

    def at_y(self, dy):
        return (self.r + 2 * dy + 8) % 8, self.c

    def x_far(self):
        return self.r, (self.c + 16) % 32

    def permuted(self):
        return (self.c + 4) % 8, self.r * 4 + self.c // 8

    def permuted_from(self):
        return self.c // 4, (self.c % 4) * 8 + (self.r + 4) % 8

    def x_far_core(self):
        return self.r, self.col(1 - self.xh, self.z, 1 - self.core)

    def x_cross(self):
        return self.y * 2 + (1 - self.xl), (self.c + 16) % 32

    def x_near(self):
        return self.y * 2 + (1 - self.xl), self.c

    def other_core(self):
        return self.r, self.c + self.sign


class Net:
    def __init__(self, send_sem, recv_sem):
        self.send_sem, self.recv_sem = send_sem, recv_sem
        self.copies = {}

    def send(self, key, src, dst, device):
        n = len(self.copies)
        copy = pltpu.make_async_remote_copy(
            src_ref=src,
            dst_ref=dst,
            send_sem=self.send_sem.at[n],
            recv_sem=self.recv_sem.at[n],
            device_id=device,
            device_id_type=pl.DeviceIdType.MESH,
        )
        copy.start()
        self.copies[key] = [copy, False]

    def wait(self, key):
        entry = self.copies[key]
        assert not entry[1]
        entry[0].wait_recv()
        entry[1] = True

    def finish(self):
        for copy, received in self.copies.values():
            assert received
            copy.wait_send()


def greet(devices):
    barrier = pltpu.get_barrier_semaphore()
    for device in devices:
        pl.semaphore_signal(barrier, inc=1, device_id=device, device_id_type=pl.DeviceIdType.MESH)
    pl.semaphore_wait(barrier, len(devices))


def reduce_slopes(me, net, a_ref, d_ref, response, a4, dg, sb, rb, sf, rf):
    r, z, xh, core, sign = me.r, me.z, me.xh, me.core, me.sign
    near = me.y * 2 + (1 - me.xl)

    def owner(way, hop, sgn):
        hops = len(HOPS[way])
        return (z + (sgn if way == "L" else -sgn) * (hops + 1 - hop) + 16) % 8

    net.send("d_far", d_ref, dg.at[2, r], me.x_far())
    net.send("d_near", d_ref, dg.at[0, r], me.x_near())
    net.send("d_cross", d_ref, dg.at[2, r], me.x_cross())
    net.send(("core", "d", 0), d_ref, dg.at[1, r], me.other_core())
    for o in (1, 3):
        net.send(("d", o), d_ref, dg.at[0, r], me.at_y(-o))
    net.send("a_core", a_ref.at[xh, :, 1 - core], a4.at[0], me.other_core())
    for way, hop in A_ORDER:
        n = owner(way, hop, sign)
        net.send(("a_far", way, hop), a_ref.at[1 - xh, n, core], a4.at[1, n], me.x_far())
        n = owner(way, hop, -sign)
        net.send(("a_cross", way, hop), a_ref.at[1 - xh, n, 1 - core], a4.at[2, n], me.x_far_core())
    dg[0, r] = d_ref[...]
    def y_of(f):
        return (me.y + Y_ORDER[f]) % 4

    pieces_of = (("d", 0, me.xl), ("d_near", 0, 1 - me.xl), ("d_cross", 2, 1 - me.xl), ("d_far", 2, me.xl))

    def from_x(key, k, row):
        def act():
            net.wait(key)
            piece = dg.at[k, row]
            for o in (1, 3):
                net.send((key, o), piece, piece, me.at_y(-o))
            net.send(("core", key, 0), piece, dg.at[k + 1, row], me.other_core())

        return act

    def from_y(key, k, side, o):
        def act():
            net.wait((key, o))
            row = (me.y + o) % 4 * 2 + side
            piece = dg.at[k, row]
            if (o, k) in ((3, 0), (1, 2)):
                net.send((key, 2), piece, piece, me.at_y(1 if o == 3 else -1))
            net.send(("core", key, o), piece, dg.at[k + 1, row], me.other_core())

        return act

    def commands_in(f):
        for key, _, _ in pieces_of:
            net.wait(("core", key, Y_ORDER[f]))
        if f == 0:
            net.wait("a_core")

    arrived = set()

    def product(f, pieces):
        for piece in pieces:
            if piece not in arrived:
                arrived.add(piece)
                net.wait(("a_far",) + piece)
                net.wait(("a_cross",) + piece)
        owners = [owner(way, hop, sign) for way, hop in pieces]
        total = None
        for k in range(4):
            if k == 0:
                rows = [a_ref[xh, n, core] for n in owners]
            else:
                rows = [a4[k - 1, n] for n in owners]
            part = lax.dot_general(
                jnp.concatenate(rows, axis=0),
                dg[k, pl.ds(y_of(f) * 2, 2)].reshape(CHUNK, 256),
                (((1,), (1,)), ((), ())),
                preferred_element_type=F32,
            )
            total = part if total is None else total + part
        return [total[i * 64 : (i + 1) * 64] for i in range(len(pieces))]

    slots = {}
    for way, kinds in HOPS.items():
        for hop, kind in enumerate(kinds, 1):
            slots[way, hop] = (kind, sum(1 for k, _ in slots.values() if k is kind))

    def buffer(f, way, hop, sending):
        kind, n = slots[way, hop]
        if kind is BF:
            return (sb if sending else rb).at[f, n]
        return (sf if sending else rf).at[f, n]

    def stage(f, hop):
        if hop == 1:
            commands_in(f)
        pieces = [(way, hop) for way in HOPS if hop <= len(HOPS[way])]
        for (way, _), value in zip(pieces, product(f, pieces)):
            step = sign if way == "L" else -sign
            if hop > 1:
                net.wait((f, way, hop - 1))
                value += buffer(f, way, hop - 1, False)[...].astype(F32)
            out = buffer(f, way, hop, True)
            out[...] = value.astype(HOPS[way][hop - 1])
            net.send((f, way, hop), out, buffer(f, way, hop, False), me.at_z(step))

    def total(f):
        (value,) = product(f, [("L", 5)])
        for way in ("S", "L"):
            net.wait((f, way, len(HOPS[way])))
            value += buffer(f, way, len(HOPS[way]), False)[...].astype(F32)
        start = pl.multiple_of(MARGIN + y_of(f) * CHUNK, CHUNK)
        response[:, pl.ds(start, CHUNK)] = value

    events = []

    def on(time, act):
        events.append((time, len(events), act))

    on(4.0, from_x("d_near", 0, near))
    on(4.2, from_x("d_cross", 2, near))
    on(6.0, from_x("d_far", 2, r))
    for o in (1, 3):
        for time, (key, k, side) in zip((4.5, 8.2, 9.0, 11.0), pieces_of):
            on(time, from_y(key, k, side, o))
    for time, (key, k, side) in zip((8.4, 12.0, 13.0, 15.0), pieces_of):
        on(time, from_y(key, k, side, 2))
    for f, begin in enumerate(CHUNK_START):
        for hop in range(1, 5):
            on(begin + HOP_TIME * (hop - 1), lambda f=f, hop=hop: stage(f, hop))
        on(begin + HOP_TIME * 4, lambda f=f: total(f))
    for _, _, act in sorted(events, key=lambda e: e[:2]):
        act()


def open_loop(response, s_ref, lag_ref, count_ref, o_ref, osh_ref):
    window = response[...]
    lag = jnp.full(window.shape, lag_ref[0], jnp.int32)
    for bit in range(MARGIN.bit_length()):
        moved = pltpu.roll(window, 1 << bit, 1)
        window = jnp.where((lag & (1 << bit)) != 0, moved, window)
    summed = window[:, MARGIN:] + s_ref[...].astype(F32)
    frame = lax.broadcasted_iota(jnp.int32, summed.shape, 1)
    count = jnp.full(summed.shape, count_ref[0], jnp.int32)
    value = jnp.where(frame < count, summed, 0.0).astype(BF)
    frames = o_ref.shape[1]
    o_ref[...] = value[:, :frames]
    later = pltpu.roll(value.astype(F32), 1, 1)
    osh_ref[...] = jnp.where(frame == 0, 0.0, later).astype(BF)[:, :frames]


def gather_slopes(me, net, o_ref, osh_ref, rows_ref, cols_ref):
    r, c, z, xh = me.r, me.c, me.z, me.xh
    target = me.permuted()
    first, second = pl.ds(0, 32), pl.ds(32, 32)
    hops = {"L": 4, "S": 3}
    step = {"L": me.sign, "S": -me.sign}

    def slot(other, dz):
        return me.col((1 - xh) if other else xh, (z + dz + 16) % 8, me.core)

    def pass_on(key, n, half, device):
        piece = rows_ref.at[n, half]
        net.send(key, piece, piece, device)

    near = me.y * 2 + (1 - me.xl)
    halves = (first, second)

    def to_core(key, n):
        net.send(key, rows_ref.at[n], rows_ref.at[n], me.other_core())

    def pass_col(key, row, half, device):
        piece = cols_ref.at[(row + 4) % 8, half]
        net.send(key, piece, piece, device)

    net.send("x1", o_ref.at[first], rows_ref.at[c, first], me.x_far())
    for p, half in enumerate(halves):
        net.send(("permute", p), osh_ref.at[half], cols_ref.at[c % 8, half], target)
    for way in hops:
        net.send(("z2", way, 1), o_ref.at[second], rows_ref.at[c, second], me.at_z(step[way]))
    for way in hops:
        net.send(("z1", way, 1), o_ref.at[first], rows_ref.at[c, first], me.at_z(step[way]))
    net.send(("x2", "own", 0), o_ref.at[second], rows_ref.at[c, second], me.x_far())
    net.send("core_own", o_ref, rows_ref.at[c], me.other_core())
    rows_ref[c] = o_ref[...]

    events = []

    def on(time, key, act=None):
        events.append((time, len(events), key, act))

    def relay(kind, half, way, t):
        def act():
            n = slot(kind == "z1p", -step[way] * t)
            if t < hops[way]:
                pass_on((kind, way, t + 1), n, half, me.at_z(step[way]))
            if kind == "z2":
                pass_on(("x2", way, t), n, second, me.x_far())
            if kind == "z1":
                to_core(("core", way, t), n)

        return act

    def cross_over():
        for way in hops:
            pass_on(("z1p", way, 1), slot(True, 0), first, me.at_z(step[way]))

    def far(way, t):
        n = slot(True, 0 if t == 0 else -step[way] * t)
        return lambda: to_core(("core_far", way, t), n)

    on(4, "x1", cross_over)
    on(12, ("x2", "own", 0), far("own", 0))
    for t in range(1, 5):
        for way in hops:
            if t <= hops[way]:
                on(4 * t, ("z2", way, t), relay("z2", second, way, t))
                on(4 * t + 1, ("z1", way, t), relay("z1", first, way, t))
                on(4 * t + 4.5, ("z1p", way, t), relay("z1p", first, way, t))
                on(4 * t + 7, ("x2", way, t), far(way, t))
    for p, half in enumerate(halves):
        def spread(p=p, half=half):
            pass_col(("near", p), r, half, me.x_near())
            for d in (1, -1):
                pass_col(("y0", p, d), r, half, me.at_y(d))

        def spread_near(p=p, half=half):
            for d in (1, -1):
                pass_col(("y1", p, d), near, half, me.at_y(d))

        late = 2 * p + COL_LATE
        on(9 + late, ("permute", p), spread)
        on(13 + late, ("near", p), spread_near)
        on(14 + late, ("y0", p, 1), lambda p=p, half=half: pass_col(("y2", p, 1), (r + 6) % 8, half, me.at_y(1)))
        on(18 + late, ("y1", p, -1), lambda p=p, half=half: pass_col(("y2", p, -1), (near + 2) % 8, half, me.at_y(-1)))
    for _, _, key, act in sorted(events, key=lambda e: e[:2]):
        net.wait(key)
        if act is not None:
            act()
    for key, entry in net.copies.items():
        if not entry[1]:
            net.wait(key)


def kernel(
    a_ref, d_ref, s_ref, lag_ref, count_ref, rows_ref, cols_ref,
    response, o_scr, osh_scr, a4, dg, sb, rb, sf, rf, send_sem, recv_sem,
):
    me = Place()
    greet(
        [me.other_core(), me.x_near(), me.x_far(), me.x_cross(), me.x_far_core(), me.at_z(1), me.at_z(-1)]
        + [me.at_y(1), me.at_y(-1), me.permuted(), me.permuted_from()]
    )
    net = Net(send_sem, recv_sem)
    response[:, :MARGIN] = jnp.zeros((64, MARGIN), F32)
    reduce_slopes(me, net, a_ref, d_ref, response, a4, dg, sb, rb, sf, rf)
    open_loop(response, s_ref, lag_ref, count_ref, o_scr, osh_scr)
    gather_slopes(me, net, o_scr, osh_scr, rows_ref, cols_ref)
    net.finish()


def gathered(number, frames, interaction, commands, slopes_measured, frame_lag, frame_count):
    kinds = [kind for way in HOPS.values() for kind in way]
    n_bf, n_f32 = kinds.count(BF), kinds.count(F32)
    piece = (64, CHUNK)
    copies = 160
    smem = pl.BlockSpec(memory_space=pltpu.SMEM)
    return pl.pallas_call(
        kernel,
        out_shape=(
            jax.ShapeDtypeStruct((32, 64, frames), BF),
            jax.ShapeDtypeStruct((8, 64, frames), BF),
        ),
        in_specs=[VMEM, VMEM, VMEM, smem, smem],
        out_specs=(VMEM, VMEM),
        scratch_shapes=[
            pltpu.VMEM((64, MARGIN + FRAMES), F32),
            pltpu.VMEM((64, frames), BF),
            pltpu.VMEM((64, frames), BF),
            pltpu.VMEM((3, 8, 64, 256), BF),
            pltpu.VMEM((4, 8, 128, 256), BF),
            pltpu.VMEM((CHUNKS, n_bf) + piece, BF),
            pltpu.VMEM((CHUNKS, n_bf) + piece, BF),
            pltpu.VMEM((CHUNKS, n_f32) + piece, F32),
            pltpu.VMEM((CHUNKS, n_f32) + piece, F32),
            pltpu.SemaphoreType.DMA((copies,)),
            pltpu.SemaphoreType.DMA((copies,)),
        ],
        compiler_params=pltpu.CompilerParams(
            collective_id=number, has_side_effects=True, vmem_limit_bytes=24 * 2**20
        ),
        name=f"open_loop_slopes_{frames}",
    )(interaction.reshape(2, 8, 2, 64, 256), commands, slopes_measured, frame_lag, frame_count)


def covariance(number, *args):
    frames = BOUNDS[number]
    rows, cols = gathered(number, frames, *args)
    tile = lax.dot_general(
        rows.reshape(2048, frames),
        cols.reshape(512, frames),
        (((1,), (1,)), ((), ())),
        preferred_element_type=F32,
    )
    return tile * (1.0 / math.sqrt(FRAMES))


def local(interaction, commands, slopes_measured, frame_lag, frame_count):
    which = sum((frame_count[0] > bound).astype(jnp.int32) for bound in BOUNDS[:-1])
    return lax.switch(
        which,
        [functools.partial(covariance, n) for n in range(len(BOUNDS))],
        interaction, commands, slopes_measured, frame_lag, frame_count,
    )


def solution(mesh):
    return jax.shard_map(
        local,
        mesh=mesh,
        in_specs=(P("rows", "cols"), P("rows", "cols"), P(("rows", "cols"), None), P(), P()),
        out_specs=P("rows", "cols"),
        check_vma=False,
    )
```

```python
import functools
import math

import jax
import jax.numpy as jnp
from jax import lax
from jax.experimental import pallas as pl
from jax.experimental.pallas import tpu as pltpu
from jax.sharding import PartitionSpec as P

FRAMES = 1024
CHUNK = 256
BOUNDS = (512, 768, 1024)
MARGIN = FRAMES // 4
CHUNKS = FRAMES // CHUNK
BF, F32 = jnp.bfloat16, jnp.float32
VMEM = pl.BlockSpec(memory_space=pltpu.VMEM)
Y_ORDER = (0, 1, 3, 2)
HOPS = {
    "L4": (4, 2, BF, 1, ()),
    "L3": (3, 1, BF, 1, ()),
    "S3": (-3, -2, BF, 1, ()),
    "S2": (-2, -1, BF, 1, ()),
    "L2": (2, 1, BF, 2, ("L4", "L3")),
    "S1": (-1, -1, F32, 2, ("S3", "S2")),
    "L1": (1, 1, F32, 3, ("L2",)),
}
STAGES = 3
A_ORDER = (4, 3, -3, -2, 2, -1, 1, 0)
CHUNK_START = (10.5, 13.0, 13.1, 15.5)
HOP_TIME = 4.0
COL_LATE = -5.0


class Place:
    def __init__(self):
        self.r = lax.axis_index("rows")
        self.c = lax.axis_index("cols")
        self.y, self.xl = self.r // 2, self.r % 2
        self.xh, self.z, self.core = self.c // 16, (self.c // 2) % 8, self.c % 2
        self.sign = 1 - 2 * self.core

    def col(self, xh, z, core):
        return xh * 16 + z * 2 + core

    def at_z(self, dz):
        return self.r, self.col(self.xh, (self.z + dz + 16) % 8, self.core)

    def at_y(self, dy):
        return (self.r + 2 * dy + 8) % 8, self.c

    def x_far(self):
        return self.r, (self.c + 16) % 32

    def permuted(self):
        return (self.c + 4) % 8, self.r * 4 + self.c // 8

    def permuted_from(self):
        return self.c // 4, (self.c % 4) * 8 + (self.r + 4) % 8

    def x_far_core(self):
        return self.r, self.col(1 - self.xh, self.z, 1 - self.core)

    def x_cross(self):
        return self.y * 2 + (1 - self.xl), (self.c + 16) % 32

    def x_near(self):
        return self.y * 2 + (1 - self.xl), self.c

    def other_core(self):
        return self.r, self.c + self.sign


class Net:
    def __init__(self, send_sem, recv_sem):
        self.send_sem, self.recv_sem = send_sem, recv_sem
        self.copies = {}

    def send(self, key, src, dst, device):
        n = len(self.copies)
        copy = pltpu.make_async_remote_copy(
            src_ref=src,
            dst_ref=dst,
            send_sem=self.send_sem.at[n],
            recv_sem=self.recv_sem.at[n],
            device_id=device,
            device_id_type=pl.DeviceIdType.MESH,
        )
        copy.start()
        self.copies[key] = [copy, False]

    def wait(self, key):
        entry = self.copies[key]
        assert not entry[1]
        entry[0].wait_recv()
        entry[1] = True

    def finish(self):
        for copy, received in self.copies.values():
            assert received
            copy.wait_send()


def greet(devices):
    barrier = pltpu.get_barrier_semaphore()
    for device in devices:
        pl.semaphore_signal(barrier, inc=1, device_id=device, device_id_type=pl.DeviceIdType.MESH)
    pl.semaphore_wait(barrier, len(devices))


def reduce_slopes(me, net, a_ref, d_ref, response, a4, dg, sb, rb, sf, rf):
    r, z, xh, core, sign = me.r, me.z, me.xh, me.core, me.sign
    near = me.y * 2 + (1 - me.xl)

    def place(ahead, sgn):
        return (z + sgn * ahead + 16) % 8

    net.send("d_far", d_ref, dg.at[2, r], me.x_far())
    net.send("d_near", d_ref, dg.at[0, r], me.x_near())
    net.send("d_cross", d_ref, dg.at[2, r], me.x_cross())
    net.send(("core", "d", 0), d_ref, dg.at[1, r], me.other_core())
    for o in (2, 1, 3):
        net.send(("d", o), d_ref, dg.at[0, r], me.at_y(-o))
    net.send("a_core", a_ref.at[xh, :, 1 - core], a4.at[0], me.other_core())

    def send_rows(places):
        for ahead in places:
            n = place(ahead, sign)
            net.send(("a_far", ahead), a_ref.at[1 - xh, n, core], a4.at[1, n], me.x_far())
            n = place(ahead, -sign)
            net.send(("a_cross", ahead), a_ref.at[1 - xh, n, 1 - core], a4.at[2, n], me.x_far_core())

    send_rows(A_ORDER[:4])
    dg[0, r] = d_ref[...]
    def y_of(f):
        return (me.y + Y_ORDER[f]) % 4

    pieces_of = (("d", 0, me.xl), ("d_near", 0, 1 - me.xl), ("d_cross", 2, 1 - me.xl), ("d_far", 2, me.xl))

    def from_x(key, k, row):
        def act():
            net.wait(key)
            piece = dg.at[k, row]
            for o in (1, 3):
                net.send((key, o), piece, piece, me.at_y(-o))
            net.send(("core", key, 0), piece, dg.at[k + 1, row], me.other_core())

        return act

    def from_y(key, k, side, o):
        def act():
            net.wait((key, o))
            row = (me.y + o) % 4 * 2 + side
            piece = dg.at[k, row]
            if (o, key) == (2, "d"):
                net.send(("d_far", 2), piece, dg.at[2, row], me.x_far())
                net.send(("d_near", 2), piece, piece, me.x_near())
                net.send(("d_cross", 2), piece, dg.at[2, row], me.x_cross())
                send_rows(A_ORDER[4:])
            net.send(("core", key, o), piece, dg.at[k + 1, row], me.other_core())

        return act

    def commands_in(f):
        for key, _, _ in pieces_of:
            net.wait(("core", key, Y_ORDER[f]))
        if f == 0:
            net.wait("a_core")

    arrived = set()

    def product(f, places):
        for ahead in places:
            if ahead not in arrived:
                arrived.add(ahead)
                net.wait(("a_far", ahead))
                net.wait(("a_cross", ahead))
        owners = [place(ahead, sign) for ahead in places]
        total = None
        for k in range(4):
            if k == 0:
                rows = [a_ref[xh, n, core] for n in owners]
            else:
                rows = [a4[k - 1, n] for n in owners]
            part = lax.dot_general(
                jnp.concatenate(rows, axis=0),
                dg[k, pl.ds(y_of(f) * 2, 2)].reshape(CHUNK, 256),
                (((1,), (1,)), ((), ())),
                preferred_element_type=F32,
            )
            total = part if total is None else total + part
        return [total[i * 64 : (i + 1) * 64] for i in range(len(places))]

    slots = {}
    for name, (_, _, kind, _, _) in HOPS.items():
        slots[name] = (kind, sum(1 for k, _ in slots.values() if k is kind))

    def buffer(f, name, sending):
        kind, n = slots[name]
        if kind is BF:
            return (sb if sending else rb).at[f, n]
        return (sf if sending else rf).at[f, n]

    def plus_received(f, value, names):
        for name in names:
            net.wait((f, name))
            value += buffer(f, name, False)[...].astype(F32)
        return value

    def stage(f, number):
        if number == 1:
            commands_in(f)
        names = [name for name, hop in HOPS.items() if hop[3] == number]
        for name, value in zip(names, product(f, [HOPS[name][0] for name in names])):
            _, to, kind, _, received = HOPS[name]
            out = buffer(f, name, True)
            out[...] = plus_received(f, value, received).astype(kind)
            net.send((f, name), out, buffer(f, name, False), me.at_z(sign * to))

    def total(f):
        (value,) = product(f, [0])
        value = plus_received(f, value, ("S1", "L1"))
        start = pl.multiple_of(MARGIN + y_of(f) * CHUNK, CHUNK)
        response[:, pl.ds(start, CHUNK)] = value

    events = []

    def on(time, act):
        events.append((time, len(events), act))

    on(4.0, from_x("d_near", 0, near))
    on(4.2, from_x("d_cross", 2, near))
    on(6.0, from_x("d_far", 2, r))
    for o, times in ((1, (4.5, 8.2, 9.0, 11.0)), (3, (4.5, 8.2, 9.0, 11.0)), (2, (5.0, 12.2, 12.4, 13.5))):
        for time, (key, k, side) in zip(times, pieces_of):
            on(time, from_y(key, k, side, o))
    for f, begin in enumerate(CHUNK_START):
        for number in range(1, STAGES + 1):
            on(begin + HOP_TIME * (number - 1), lambda f=f, number=number: stage(f, number))
        on(begin + HOP_TIME * STAGES, lambda f=f: total(f))
    for _, _, act in sorted(events, key=lambda e: e[:2]):
        act()


def open_loop(response, s_ref, lag_ref, count_ref, o_ref, osh_ref):
    window = response[...]
    lag = jnp.full(window.shape, lag_ref[0], jnp.int32)
    for bit in range(MARGIN.bit_length()):
        moved = pltpu.roll(window, 1 << bit, 1)
        window = jnp.where((lag & (1 << bit)) != 0, moved, window)
    summed = window[:, MARGIN:] + s_ref[...].astype(F32)
    frame = lax.broadcasted_iota(jnp.int32, summed.shape, 1)
    count = jnp.full(summed.shape, count_ref[0], jnp.int32)
    value = jnp.where(frame < count, summed, 0.0).astype(BF)
    frames = o_ref.shape[1]
    o_ref[...] = value[:, :frames]
    later = pltpu.roll(value.astype(F32), 1, 1)
    osh_ref[...] = jnp.where(frame == 0, 0.0, later).astype(BF)[:, :frames]


def gather_slopes(me, net, o_ref, osh_ref, rows_ref, cols_ref):
    r, c, z, xh = me.r, me.c, me.z, me.xh
    target = me.permuted()
    first, second = pl.ds(0, 32), pl.ds(32, 32)
    hops = {"L": 4, "S": 3}
    step = {"L": me.sign, "S": -me.sign}

    def slot(other, dz):
        return me.col((1 - xh) if other else xh, (z + dz + 16) % 8, me.core)

    def pass_on(key, n, half, device):
        piece = rows_ref.at[n, half]
        net.send(key, piece, piece, device)

    near = me.y * 2 + (1 - me.xl)
    halves = (first, second)

    def to_core(key, n):
        net.send(key, rows_ref.at[n], rows_ref.at[n], me.other_core())

    def pass_col(key, row, half, device):
        piece = cols_ref.at[(row + 4) % 8, half]
        net.send(key, piece, piece, device)

    net.send("x1", o_ref.at[first], rows_ref.at[c, first], me.x_far())
    for p, half in enumerate(halves):
        net.send(("permute", p), osh_ref.at[half], cols_ref.at[c % 8, half], target)
    for way in hops:
        net.send(("z2", way, 1), o_ref.at[second], rows_ref.at[c, second], me.at_z(step[way]))
    for way in hops:
        net.send(("z1", way, 1), o_ref.at[first], rows_ref.at[c, first], me.at_z(step[way]))
    net.send(("x2", "own", 0), o_ref.at[second], rows_ref.at[c, second], me.x_far())
    net.send("core_own", o_ref, rows_ref.at[c], me.other_core())
    rows_ref[c] = o_ref[...]

    events = []

    def on(time, key, act=None):
        events.append((time, len(events), key, act))

    def relay(kind, half, way, t):
        def act():
            n = slot(kind == "z1p", -step[way] * t)
            if t < hops[way]:
                pass_on((kind, way, t + 1), n, half, me.at_z(step[way]))
            if kind == "z2":
                pass_on(("x2", way, t), n, second, me.x_far())
            if kind == "z1":
                to_core(("core", way, t), n)

        return act

    def cross_over():
        for way in hops:
            pass_on(("z1p", way, 1), slot(True, 0), first, me.at_z(step[way]))

    def far(way, t):
        n = slot(True, 0 if t == 0 else -step[way] * t)
        return lambda: to_core(("core_far", way, t), n)

    on(4, "x1", cross_over)
    on(12, ("x2", "own", 0), far("own", 0))
    for t in range(1, 5):
        for way in hops:
            if t <= hops[way]:
                on(4 * t, ("z2", way, t), relay("z2", second, way, t))
                on(4 * t + 1, ("z1", way, t), relay("z1", first, way, t))
                on(4 * t + 4.5, ("z1p", way, t), relay("z1p", first, way, t))
                on(4 * t + 7, ("x2", way, t), far(way, t))
    for p, half in enumerate(halves):
        def spread(p=p, half=half):
            pass_col(("near", p), r, half, me.x_near())
            for d in (1, -1):
                pass_col(("y0", p, d), r, half, me.at_y(d))

        def spread_near(p=p, half=half):
            for d in (1, -1):
                pass_col(("y1", p, d), near, half, me.at_y(d))

        late = 2 * p + COL_LATE
        on(9 + late, ("permute", p), spread)
        on(13 + late, ("near", p), spread_near)
        on(14 + late, ("y0", p, 1), lambda p=p, half=half: pass_col(("y2", p, 1), (r + 6) % 8, half, me.at_y(1)))
        on(18 + late, ("y1", p, -1), lambda p=p, half=half: pass_col(("y2", p, -1), (near + 2) % 8, half, me.at_y(-1)))
    for _, _, key, act in sorted(events, key=lambda e: e[:2]):
        net.wait(key)
        if act is not None:
            act()
    for key, entry in net.copies.items():
        if not entry[1]:
            net.wait(key)


def kernel(
    a_ref, d_ref, s_ref, lag_ref, count_ref, rows_ref, cols_ref,
    response, o_scr, osh_scr, a4, dg, sb, rb, sf, rf, send_sem, recv_sem,
):
    me = Place()
    greet(
        [me.other_core(), me.x_near(), me.x_far(), me.x_cross(), me.x_far_core(), me.at_z(1), me.at_z(-1)]
        + [me.at_z(2), me.at_z(-2), me.at_y(1), me.at_y(-1), me.at_y(2), me.permuted(), me.permuted_from()]
    )
    net = Net(send_sem, recv_sem)
    response[:, :MARGIN] = jnp.zeros((64, MARGIN), F32)
    reduce_slopes(me, net, a_ref, d_ref, response, a4, dg, sb, rb, sf, rf)
    open_loop(response, s_ref, lag_ref, count_ref, o_scr, osh_scr)
    gather_slopes(me, net, o_scr, osh_scr, rows_ref, cols_ref)
    net.finish()


def gathered(number, frames, interaction, commands, slopes_measured, frame_lag, frame_count):
    kinds = [hop[2] for hop in HOPS.values()]
    n_bf, n_f32 = kinds.count(BF), kinds.count(F32)
    piece = (64, CHUNK)
    copies = 160
    smem = pl.BlockSpec(memory_space=pltpu.SMEM)
    return pl.pallas_call(
        kernel,
        out_shape=(
            jax.ShapeDtypeStruct((32, 64, frames), BF),
            jax.ShapeDtypeStruct((8, 64, frames), BF),
        ),
        in_specs=[VMEM, VMEM, VMEM, smem, smem],
        out_specs=(VMEM, VMEM),
        scratch_shapes=[
            pltpu.VMEM((64, MARGIN + FRAMES), F32),
            pltpu.VMEM((64, frames), BF),
            pltpu.VMEM((64, frames), BF),
            pltpu.VMEM((3, 8, 64, 256), BF),
            pltpu.VMEM((4, 8, 128, 256), BF),
            pltpu.VMEM((CHUNKS, n_bf) + piece, BF),
            pltpu.VMEM((CHUNKS, n_bf) + piece, BF),
            pltpu.VMEM((CHUNKS, n_f32) + piece, F32),
            pltpu.VMEM((CHUNKS, n_f32) + piece, F32),
            pltpu.SemaphoreType.DMA((copies,)),
            pltpu.SemaphoreType.DMA((copies,)),
        ],
        compiler_params=pltpu.CompilerParams(
            collective_id=number, has_side_effects=True, vmem_limit_bytes=24 * 2**20
        ),
        name=f"open_loop_slopes_{frames}",
    )(interaction.reshape(2, 8, 2, 64, 256), commands, slopes_measured, frame_lag, frame_count)


def covariance(number, *args):
    frames = BOUNDS[number]
    rows, cols = gathered(number, frames, *args)
    tile = lax.dot_general(
        rows.reshape(2048, frames),
        cols.reshape(512, frames),
        (((1,), (1,)), ((), ())),
        preferred_element_type=F32,
    )
    return tile * (1.0 / math.sqrt(FRAMES))


def local(interaction, commands, slopes_measured, frame_lag, frame_count):
    which = sum((frame_count[0] > bound).astype(jnp.int32) for bound in BOUNDS[:-1])
    return lax.switch(
        which,
        [functools.partial(covariance, n) for n in range(len(BOUNDS))],
        interaction, commands, slopes_measured, frame_lag, frame_count,
    )


def solution(mesh):
    return jax.shard_map(
        local,
        mesh=mesh,
        in_specs=(P("rows", "cols"), P("rows", "cols"), P(("rows", "cols"), None), P(), P()),
        out_specs=P("rows", "cols"),
        check_vma=False,
    )
```

```python
import functools
import math

import jax
import jax.numpy as jnp
from jax import lax
from jax.experimental import pallas as pl
from jax.experimental.pallas import tpu as pltpu
from jax.sharding import PartitionSpec as P

FRAMES = 1024
CHUNK = 256
BOUNDS = (512, 768, 1024)
MARGIN = FRAMES // 4
CHUNKS = FRAMES // CHUNK
BF, F32 = jnp.bfloat16, jnp.float32
VMEM = pl.BlockSpec(memory_space=pltpu.VMEM)
Y_ORDER = (0, 1, 3, 2)
HOPS = {
    "L4": (4, 2, BF, 1, ()),
    "L3": (3, 1, BF, 1, ()),
    "S3": (-3, -2, BF, 1, ()),
    "S2": (-2, -1, BF, 1, ()),
    "L2": (2, 1, BF, 2, ("L4", "L3")),
    "S1": (-1, -1, F32, 2, ("S3", "S2")),
    "L1": (1, 1, F32, 3, ("L2",)),
}
STAGES = 3
A_ORDER = (4, 3, -3, -2, 2, -1, 1, 0)
CHUNK_START = (10.5, 13.0, 13.1, 15.5)
HOP_TIME = 4.0
COL_LATE = -5.0


class Place:
    def __init__(self):
        self.r = lax.axis_index("rows")
        self.c = lax.axis_index("cols")
        self.y, self.xl = self.r // 2, self.r % 2
        self.xh, self.z, self.core = self.c // 16, (self.c // 2) % 8, self.c % 2
        self.sign = 1 - 2 * self.core

    def col(self, xh, z, core):
        return xh * 16 + z * 2 + core

    def at_z(self, dz):
        return self.r, self.col(self.xh, (self.z + dz + 16) % 8, self.core)

    def at_y(self, dy):
        return (self.r + 2 * dy + 8) % 8, self.c

    def x_far(self):
        return self.r, (self.c + 16) % 32

    def permuted(self):
        return (self.c + 4) % 8, self.r * 4 + self.c // 8

    def permuted_from(self):
        return self.c // 4, (self.c % 4) * 8 + (self.r + 4) % 8

    def x_far_core(self):
        return self.r, self.col(1 - self.xh, self.z, 1 - self.core)

    def x_cross(self):
        return self.y * 2 + (1 - self.xl), (self.c + 16) % 32

    def x_near(self):
        return self.y * 2 + (1 - self.xl), self.c

    def other_core(self):
        return self.r, self.c + self.sign


class Net:
    def __init__(self, send_sem, recv_sem):
        self.send_sem, self.recv_sem = send_sem, recv_sem
        self.copies = {}

    def send(self, key, src, dst, device):
        n = len(self.copies)
        copy = pltpu.make_async_remote_copy(
            src_ref=src,
            dst_ref=dst,
            send_sem=self.send_sem.at[n],
            recv_sem=self.recv_sem.at[n],
            device_id=device,
            device_id_type=pl.DeviceIdType.MESH,
        )
        copy.start()
        self.copies[key] = [copy, False]

    def wait(self, key):
        entry = self.copies[key]
        assert not entry[1]
        entry[0].wait_recv()
        entry[1] = True

    def finish(self):
        for copy, received in self.copies.values():
            assert received
            copy.wait_send()


def greet(devices):
    barrier = pltpu.get_barrier_semaphore()
    for device in devices:
        pl.semaphore_signal(barrier, inc=1, device_id=device, device_id_type=pl.DeviceIdType.MESH)
    pl.semaphore_wait(barrier, len(devices))


def reduce_slopes(me, net, a_ref, d_ref, response, a4, dg, sb, rb, sf, rf):
    r, z, xh, core, sign = me.r, me.z, me.xh, me.core, me.sign
    near = me.y * 2 + (1 - me.xl)

    def place(ahead, sgn):
        return (z + sgn * ahead + 16) % 8

    net.send("d_far", d_ref, dg.at[2, r], me.x_far())
    net.send("d_near", d_ref, dg.at[0, r], me.x_near())
    net.send("d_cross", d_ref, dg.at[2, r], me.x_cross())
    net.send(("core", "d", 0), d_ref, dg.at[1, r], me.other_core())
    for o in (2, 1, 3):
        net.send(("d", o), d_ref, dg.at[0, r], me.at_y(-o))
    net.send("a_core", a_ref.at[xh, :, 1 - core], a4.at[0], me.other_core())

    def send_rows(places):
        for ahead in places:
            n = place(ahead, sign)
            net.send(("a_far", ahead), a_ref.at[1 - xh, n, core], a4.at[1, n], me.x_far())
            n = place(ahead, -sign)
            net.send(("a_cross", ahead), a_ref.at[1 - xh, n, 1 - core], a4.at[2, n], me.x_far_core())

    send_rows(A_ORDER[:4])
    dg[0, r] = d_ref[...]
    def y_of(f):
        return (me.y + Y_ORDER[f]) % 4

    pieces_of = (("d", 0, me.xl), ("d_near", 0, 1 - me.xl), ("d_cross", 2, 1 - me.xl), ("d_far", 2, me.xl))

    def from_x(key, k, row):
        def act():
            net.wait(key)
            piece = dg.at[k, row]
            for o in (1, 3):
                net.send((key, o), piece, piece, me.at_y(-o))
            net.send(("core", key, 0), piece, dg.at[k + 1, row], me.other_core())

        return act

    def from_y(key, k, side, o):
        def act():
            net.wait((key, o))
            row = (me.y + o) % 4 * 2 + side
            piece = dg.at[k, row]
            if (o, key) == (2, "d"):
                net.send(("d_far", 2), piece, dg.at[2, row], me.x_far())
                net.send(("d_near", 2), piece, piece, me.x_near())
                net.send(("d_cross", 2), piece, dg.at[2, row], me.x_cross())
                send_rows(A_ORDER[4:])
            net.send(("core", key, o), piece, dg.at[k + 1, row], me.other_core())

        return act

    def commands_in(f):
        for key, _, _ in pieces_of:
            net.wait(("core", key, Y_ORDER[f]))
        if f == 0:
            net.wait("a_core")

    arrived = set()

    def product(f, places):
        for ahead in places:
            if ahead not in arrived:
                arrived.add(ahead)
                net.wait(("a_far", ahead))
                net.wait(("a_cross", ahead))
        owners = [place(ahead, sign) for ahead in places]
        total = None
        for k in range(4):
            if k == 0:
                rows = [a_ref[xh, n, core] for n in owners]
            else:
                rows = [a4[k - 1, n] for n in owners]
            part = lax.dot_general(
                jnp.concatenate(rows, axis=0),
                dg[k, pl.ds(y_of(f) * 2, 2)].reshape(CHUNK, 256),
                (((1,), (1,)), ((), ())),
                preferred_element_type=F32,
            )
            total = part if total is None else total + part
        return [total[i * 64 : (i + 1) * 64] for i in range(len(places))]

    slots = {}
    for name, (_, _, kind, _, _) in HOPS.items():
        slots[name] = (kind, sum(1 for k, _ in slots.values() if k is kind))

    def buffer(f, name, sending):
        kind, n = slots[name]
        if kind is BF:
            return (sb if sending else rb).at[f, n]
        return (sf if sending else rf).at[f, n]

    def plus_received(f, value, names):
        for name in names:
            net.wait((f, name))
            value += buffer(f, name, False)[...].astype(F32)
        return value

    def stage(f, number):
        if number == 1:
            commands_in(f)
        names = [name for name, hop in HOPS.items() if hop[3] == number]
        for name, value in zip(names, product(f, [HOPS[name][0] for name in names])):
            _, to, kind, _, received = HOPS[name]
            out = buffer(f, name, True)
            out[...] = plus_received(f, value, received).astype(kind)
            net.send((f, name), out, buffer(f, name, False), me.at_z(sign * to))

    def total(f):
        (value,) = product(f, [0])
        value = plus_received(f, value, ("S1", "L1"))
        start = pl.multiple_of(MARGIN + y_of(f) * CHUNK, CHUNK)
        response[:, pl.ds(start, CHUNK)] = value

    events = []

    def on(time, act):
        events.append((time, len(events), act))

    on(4.0, from_x("d_near", 0, near))
    on(4.2, from_x("d_cross", 2, near))
    on(6.0, from_x("d_far", 2, r))
    for o, times in ((1, (4.5, 8.2, 9.0, 11.0)), (3, (4.5, 8.2, 9.0, 11.0)), (2, (5.0, 12.2, 12.4, 13.5))):
        for time, (key, k, side) in zip(times, pieces_of):
            on(time, from_y(key, k, side, o))
    for f, begin in enumerate(CHUNK_START):
        for number in range(1, STAGES + 1):
            on(begin + HOP_TIME * (number - 1), lambda f=f, number=number: stage(f, number))
        on(begin + HOP_TIME * STAGES, lambda f=f: total(f))
    for _, _, act in sorted(events, key=lambda e: e[:2]):
        act()


def open_loop(response, s_ref, lag_ref, count_ref, o_ref, osh_ref):
    window = response[...]
    lag = jnp.full(window.shape, lag_ref[0], jnp.int32)
    for bit in range(MARGIN.bit_length()):
        moved = pltpu.roll(window, 1 << bit, 1)
        window = jnp.where((lag & (1 << bit)) != 0, moved, window)
    summed = window[:, MARGIN:] + s_ref[...].astype(F32)
    frame = lax.broadcasted_iota(jnp.int32, summed.shape, 1)
    count = jnp.full(summed.shape, count_ref[0], jnp.int32)
    value = jnp.where(frame < count, summed, 0.0).astype(BF)
    frames = o_ref.shape[1]
    o_ref[...] = value[:, :frames]
    later = pltpu.roll(value.astype(F32), 1, 1)
    osh_ref[...] = jnp.where(frame == 0, 0.0, later).astype(BF)[:, :frames]


def gather_slopes(me, net, o_ref, osh_ref, rows_ref, cols_ref):
    r, c, z, xh = me.r, me.c, me.z, me.xh
    target = me.permuted()
    first, second = pl.ds(0, 32), pl.ds(32, 32)
    hops = {"L": 4, "S": 3}
    step = {"L": me.sign, "S": -me.sign}

    def slot(other, dz):
        return me.col((1 - xh) if other else xh, (z + dz + 16) % 8, me.core)

    def pass_on(key, n, half, device):
        piece = rows_ref.at[n, half]
        net.send(key, piece, piece, device)

    near = me.y * 2 + (1 - me.xl)
    halves = (first, second)

    def to_core(key, n):
        net.send(key, rows_ref.at[n], rows_ref.at[n], me.other_core())

    def pass_col(key, row, half, device):
        piece = cols_ref.at[(row + 4) % 8, half]
        net.send(key, piece, piece, device)

    net.send("x1", o_ref.at[first], rows_ref.at[c, first], me.x_far())
    for p, half in enumerate(halves):
        net.send(("permute", p), osh_ref.at[half], cols_ref.at[c % 8, half], target)
    for way in hops:
        net.send(("z2", way, 1), o_ref.at[second], rows_ref.at[c, second], me.at_z(step[way]))
    for way in hops:
        net.send(("z1", way, 1), o_ref.at[first], rows_ref.at[c, first], me.at_z(step[way]))
    net.send(("x2", "own", 0), o_ref.at[second], rows_ref.at[c, second], me.x_far())
    net.send("core_own", o_ref, rows_ref.at[c], me.other_core())
    rows_ref[c] = o_ref[...]

    events = []

    def on(time, key, act=None):
        events.append((time, len(events), key, act))

    onward = {"L": {1: ((3, 2), (2, 1)), 3: ((4, 1),)}, "S": {1: ((2, 1),), 2: ((3, 1),)}}
    arrival = {("L", 1): 4.0, ("L", 2): 8.3, ("L", 3): 8.0, ("L", 4): 12.0}
    arrival.update({("S", 1): 4.1, ("S", 2): 8.1, ("S", 3): 12.1})

    def relay(kind, half, way, t):
        def act():
            n = slot(kind == "z1p", -step[way] * t)
            for later, distance in onward[way].get(t, ()):
                pass_on((kind, way, later), n, half, me.at_z(step[way] * distance))
            if kind == "z2":
                pass_on(("x2", way, t), n, second, me.x_far())
            if kind == "z1":
                to_core(("core", way, t), n)

        return act

    def cross_over():
        for way in hops:
            pass_on(("z1p", way, 1), slot(True, 0), first, me.at_z(step[way]))

    def far(way, t):
        n = slot(True, 0 if t == 0 else -step[way] * t)
        return lambda: to_core(("core_far", way, t), n)

    on(4, "x1", cross_over)
    on(12, ("x2", "own", 0), far("own", 0))
    for t in range(1, 5):
        for way in hops:
            if t <= hops[way]:
                at = arrival[way, t]
                on(at, ("z2", way, t), relay("z2", second, way, t))
                on(at + 1, ("z1", way, t), relay("z1", first, way, t))
                on(at + 4.5, ("z1p", way, t), relay("z1p", first, way, t))
                on(at + 7, ("x2", way, t), far(way, t))
    for p, half in enumerate(halves):
        def spread(p=p, half=half):
            pass_col(("near", p), r, half, me.x_near())
            for d in (1, -1):
                pass_col(("y0", p, d), r, half, me.at_y(d))

        def spread_near(p=p, half=half):
            for d in (2, 1, -1):
                pass_col(("y1", p, d), near, half, me.at_y(d))

        late = 2 * p + COL_LATE
        on(9 + late, ("permute", p), spread)
        on(13 + late, ("near", p), spread_near)
        on(14 + late, ("y0", p, 1), lambda p=p, half=half: pass_col(("y2", p, 1), (r + 6) % 8, half, me.at_y(1)))
    for _, _, key, act in sorted(events, key=lambda e: e[:2]):
        net.wait(key)
        if act is not None:
            act()
    for key, entry in net.copies.items():
        if not entry[1]:
            net.wait(key)


def kernel(
    a_hbm, d_hbm, s_hbm, lag_ref, count_ref, rows_ref, cols_ref,
    a_ref, d_ref, s_ref, in_sem, response, o_scr, osh_scr, a4, dg, sb, rb, sf, rf, send_sem, recv_sem,
):
    me = Place()
    loads = [
        pltpu.make_async_copy(source, target, in_sem.at[n])
        for n, (source, target) in enumerate(((d_hbm, d_ref), (a_hbm, a_ref), (s_hbm, s_ref)))
    ]
    for load in loads:
        load.start()
    greet(
        [me.other_core(), me.x_near(), me.x_far(), me.x_cross(), me.x_far_core(), me.at_z(1), me.at_z(-1)]
        + [me.at_z(2), me.at_z(-2), me.at_y(1), me.at_y(-1), me.at_y(2), me.permuted(), me.permuted_from()]
    )
    net = Net(send_sem, recv_sem)
    for load in loads:
        load.wait()
    response[:, :MARGIN] = jnp.zeros((64, MARGIN), F32)
    reduce_slopes(me, net, a_ref, d_ref, response, a4, dg, sb, rb, sf, rf)
    open_loop(response, s_ref, lag_ref, count_ref, o_scr, osh_scr)
    gather_slopes(me, net, o_scr, osh_scr, rows_ref, cols_ref)
    net.finish()


def gathered(number, frames, interaction, commands, slopes_measured, frame_lag, frame_count):
    kinds = [hop[2] for hop in HOPS.values()]
    n_bf, n_f32 = kinds.count(BF), kinds.count(F32)
    piece = (64, CHUNK)
    copies = 160
    smem = pl.BlockSpec(memory_space=pltpu.SMEM)
    return pl.pallas_call(
        kernel,
        out_shape=(
            jax.ShapeDtypeStruct((32, 64, frames), BF),
            jax.ShapeDtypeStruct((8, 64, frames), BF),
        ),
        in_specs=[pl.BlockSpec(memory_space=pl.ANY)] * 3 + [smem, smem],
        out_specs=(VMEM, VMEM),
        scratch_shapes=[
            pltpu.VMEM((2, 8, 2, 64, 256), BF),
            pltpu.VMEM((128, 256), BF),
            pltpu.VMEM((64, FRAMES), BF),
            pltpu.SemaphoreType.DMA((3,)),
            pltpu.VMEM((64, MARGIN + FRAMES), F32),
            pltpu.VMEM((64, frames), BF),
            pltpu.VMEM((64, frames), BF),
            pltpu.VMEM((3, 8, 64, 256), BF),
            pltpu.VMEM((4, 8, 128, 256), BF),
            pltpu.VMEM((CHUNKS, n_bf) + piece, BF),
            pltpu.VMEM((CHUNKS, n_bf) + piece, BF),
            pltpu.VMEM((CHUNKS, n_f32) + piece, F32),
            pltpu.VMEM((CHUNKS, n_f32) + piece, F32),
            pltpu.SemaphoreType.DMA((copies,)),
            pltpu.SemaphoreType.DMA((copies,)),
        ],
        compiler_params=pltpu.CompilerParams(
            collective_id=number, has_side_effects=True, vmem_limit_bytes=24 * 2**20
        ),
        name=f"open_loop_slopes_{frames}",
    )(interaction.reshape(2, 8, 2, 64, 256), commands, slopes_measured, frame_lag, frame_count)


def covariance(number, *args):
    frames = BOUNDS[number]
    rows, cols = gathered(number, frames, *args)
    tile = lax.dot_general(
        rows.reshape(2048, frames),
        cols.reshape(512, frames),
        (((1,), (1,)), ((), ())),
        preferred_element_type=F32,
    )
    return tile * (1.0 / math.sqrt(FRAMES))


def local(interaction, commands, slopes_measured, frame_lag, frame_count):
    which = sum((frame_count[0] > bound).astype(jnp.int32) for bound in BOUNDS[:-1])
    return lax.switch(
        which,
        [functools.partial(covariance, n) for n in range(len(BOUNDS))],
        interaction, commands, slopes_measured, frame_lag, frame_count,
    )


def solution(mesh):
    return jax.shard_map(
        local,
        mesh=mesh,
        in_specs=(P("rows", "cols"), P("rows", "cols"), P(("rows", "cols"), None), P(), P()),
        out_specs=P("rows", "cols"),
        check_vma=False,
    )
```

```python
import functools
import math

import jax
import jax.numpy as jnp
from jax import lax
from jax.experimental import pallas as pl
from jax.experimental.pallas import tpu as pltpu
from jax.sharding import PartitionSpec as P

FRAMES = 1024
CHUNK = 256
BOUNDS = (512, 640, 768, 896, 1024)
MARGIN = FRAMES // 4
CHUNKS = FRAMES // CHUNK
BF, F32 = jnp.bfloat16, jnp.float32
VMEM = pl.BlockSpec(memory_space=pltpu.VMEM)
Y_ORDER = (0, 1, 3, 2)
HOPS = {
    "L4": (4, 2, BF, 1, ()),
    "L3": (3, 1, BF, 1, ()),
    "S3": (-3, -2, BF, 1, ()),
    "S2": (-2, -1, BF, 1, ()),
    "L2": (2, 1, BF, 2, ("L4", "L3")),
    "S1": (-1, -1, F32, 2, ("S3", "S2")),
    "L1": (1, 1, F32, 3, ("L2",)),
}
STAGES = 3
A_ORDER = (4, 3, -3, -2, 2, -1, 1, 0)
CHUNK_START = (9.0, 11.2, 11.3, 14.0)
HOP_TIME = 4.0
COL_LATE = -5.0


class Place:
    def __init__(self):
        self.r = lax.axis_index("rows")
        self.c = lax.axis_index("cols")
        self.y, self.xl = self.r // 2, self.r % 2
        self.xh, self.z, self.core = self.c // 16, (self.c // 2) % 8, self.c % 2
        self.sign = 1 - 2 * self.core

    def col(self, xh, z, core):
        return xh * 16 + z * 2 + core

    def at_z(self, dz):
        return self.r, self.col(self.xh, (self.z + dz + 16) % 8, self.core)

    def at_y(self, dy):
        return (self.r + 2 * dy + 8) % 8, self.c

    def x_far(self):
        return self.r, (self.c + 16) % 32

    def permuted(self):
        return (self.c + 4) % 8, self.r * 4 + self.c // 8

    def permuted_from(self):
        return self.c // 4, (self.c % 4) * 8 + (self.r + 4) % 8

    def x_far_core(self):
        return self.r, self.col(1 - self.xh, self.z, 1 - self.core)

    def x_cross(self):
        return self.y * 2 + (1 - self.xl), (self.c + 16) % 32

    def x_near(self):
        return self.y * 2 + (1 - self.xl), self.c

    def other_core(self):
        return self.r, self.c + self.sign


class Net:
    def __init__(self, send_sem, recv_sem):
        self.send_sem, self.recv_sem = send_sem, recv_sem
        self.copies = {}

    def send(self, key, src, dst, device):
        n = len(self.copies)
        copy = pltpu.make_async_remote_copy(
            src_ref=src,
            dst_ref=dst,
            send_sem=self.send_sem.at[n],
            recv_sem=self.recv_sem.at[n],
            device_id=device,
            device_id_type=pl.DeviceIdType.MESH,
        )
        copy.start()
        self.copies[key] = [copy, False]

    def wait(self, key):
        entry = self.copies[key]
        assert not entry[1]
        entry[0].wait_recv()
        entry[1] = True

    def finish(self):
        for copy, received in self.copies.values():
            assert received
            copy.wait_send()


def greet(devices):
    barrier = pltpu.get_barrier_semaphore()
    for device in devices:
        pl.semaphore_signal(barrier, inc=1, device_id=device, device_id_type=pl.DeviceIdType.MESH)
    pl.semaphore_wait(barrier, len(devices))


def reduce_slopes(me, net, a_ref, d_ref, response, a4, dg, sb, rb, sf, rf):
    r, z, xh, core, sign = me.r, me.z, me.xh, me.core, me.sign
    near = me.y * 2 + (1 - me.xl)

    def place(ahead, sgn):
        return (z + sgn * ahead + 16) % 8

    net.send("d_far", d_ref, dg.at[2, r], me.x_far())
    net.send("d_near", d_ref, dg.at[0, r], me.x_near())
    net.send("d_cross", d_ref, dg.at[2, r], me.x_cross())
    net.send(("core", "d", 0), d_ref, dg.at[1, r], me.other_core())
    for o in (2, 1, 3):
        net.send(("d", o), d_ref, dg.at[0, r], me.at_y(-o))
    net.send("a_core", a_ref.at[xh, :, 1 - core], a4.at[0], me.other_core())

    def send_rows(places):
        for ahead in places:
            n = place(ahead, sign)
            net.send(("a_far", ahead), a_ref.at[1 - xh, n, core], a4.at[1, n], me.x_far())
            n = place(ahead, -sign)
            net.send(("a_cross", ahead), a_ref.at[1 - xh, n, 1 - core], a4.at[2, n], me.x_far_core())

    send_rows(A_ORDER[:4])
    dg[0, r] = d_ref[...]
    def y_of(f):
        return (me.y + Y_ORDER[f]) % 4

    pieces_of = (("d", 0, me.xl), ("d_near", 0, 1 - me.xl), ("d_cross", 2, 1 - me.xl), ("d_far", 2, me.xl))

    def from_x(key, k, row):
        def act():
            net.wait(key)
            piece = dg.at[k, row]
            for o in (1, 3):
                net.send((key, o), piece, piece, me.at_y(-o))
            net.send(("core", key, 0), piece, dg.at[k + 1, row], me.other_core())

        return act

    def from_y(key, k, side, o):
        def act():
            net.wait((key, o))
            row = (me.y + o) % 4 * 2 + side
            piece = dg.at[k, row]
            if (o, key) == (2, "d"):
                net.send(("d_far", 2), piece, dg.at[2, row], me.x_far())
                net.send(("d_near", 2), piece, piece, me.x_near())
                net.send(("d_cross", 2), piece, dg.at[2, row], me.x_cross())
                send_rows(A_ORDER[4:])
            net.send(("core", key, o), piece, dg.at[k + 1, row], me.other_core())

        return act

    def commands_in(f):
        for key, _, _ in pieces_of:
            net.wait(("core", key, Y_ORDER[f]))
        if f == 0:
            net.wait("a_core")

    arrived = set()

    def product(f, places):
        for ahead in places:
            if ahead not in arrived:
                arrived.add(ahead)
                net.wait(("a_far", ahead))
                net.wait(("a_cross", ahead))
        owners = [place(ahead, sign) for ahead in places]
        total = None
        for k in range(4):
            if k == 0:
                rows = [a_ref[xh, n, core] for n in owners]
            else:
                rows = [a4[k - 1, n] for n in owners]
            part = lax.dot_general(
                jnp.concatenate(rows, axis=0),
                dg[k, pl.ds(y_of(f) * 2, 2)].reshape(CHUNK, 256),
                (((1,), (1,)), ((), ())),
                preferred_element_type=F32,
            )
            total = part if total is None else total + part
        return [total[i * 64 : (i + 1) * 64] for i in range(len(places))]

    slots = {}
    for name, (_, _, kind, _, _) in HOPS.items():
        slots[name] = (kind, sum(1 for k, _ in slots.values() if k is kind))

    def buffer(f, name, sending):
        kind, n = slots[name]
        if kind is BF:
            return (sb if sending else rb).at[f, n]
        return (sf if sending else rf).at[f, n]

    def plus_received(f, value, names):
        for name in names:
            net.wait((f, name))
            value += buffer(f, name, False)[...].astype(F32)
        return value

    def stage(f, number):
        if number == 1:
            commands_in(f)
        names = [name for name, hop in HOPS.items() if hop[3] == number]
        for name, value in zip(names, product(f, [HOPS[name][0] for name in names])):
            _, to, kind, _, received = HOPS[name]
            out = buffer(f, name, True)
            out[...] = plus_received(f, value, received).astype(kind)
            net.send((f, name), out, buffer(f, name, False), me.at_z(sign * to))

    def total(f):
        (value,) = product(f, [0])
        value = plus_received(f, value, ("S1", "L1"))
        start = pl.multiple_of(MARGIN + y_of(f) * CHUNK, CHUNK)
        response[:, pl.ds(start, CHUNK)] = value

    events = []

    def on(time, act):
        events.append((time, len(events), act))

    on(4.0, from_x("d_near", 0, near))
    on(4.2, from_x("d_cross", 2, near))
    on(6.0, from_x("d_far", 2, r))
    for o, times in ((1, (4.5, 8.2, 9.0, 11.0)), (3, (4.5, 8.2, 9.0, 11.0)), (2, (5.0, 12.2, 12.4, 13.5))):
        for time, (key, k, side) in zip(times, pieces_of):
            on(time, from_y(key, k, side, o))
    for f, begin in enumerate(CHUNK_START):
        for number in range(1, STAGES + 1):
            on(begin + HOP_TIME * (number - 1), lambda f=f, number=number: stage(f, number))
        on(begin + HOP_TIME * STAGES, lambda f=f: total(f))
    for _, _, act in sorted(events, key=lambda e: e[:2]):
        act()


def open_loop(response, s_ref, lag_ref, count_ref, o_ref, osh_ref):
    window = response[...]
    lag = jnp.full(window.shape, lag_ref[0], jnp.int32)
    for bit in range(MARGIN.bit_length()):
        moved = pltpu.roll(window, 1 << bit, 1)
        window = jnp.where((lag & (1 << bit)) != 0, moved, window)
    summed = window[:, MARGIN:] + s_ref[...].astype(F32)
    frame = lax.broadcasted_iota(jnp.int32, summed.shape, 1)
    count = jnp.full(summed.shape, count_ref[0], jnp.int32)
    value = jnp.where(frame < count, summed, 0.0).astype(BF)
    frames = o_ref.shape[1]
    o_ref[...] = value[:, :frames]
    later = pltpu.roll(value.astype(F32), 1, 1)
    osh_ref[...] = jnp.where(frame == 0, 0.0, later).astype(BF)[:, :frames]


def gather_slopes(me, net, o_ref, osh_ref, rows_ref, cols_ref):
    r, c, z, xh = me.r, me.c, me.z, me.xh
    target = me.permuted()
    first, second = pl.ds(0, 32), pl.ds(32, 32)
    hops = {"L": 4, "S": 3}
    step = {"L": me.sign, "S": -me.sign}

    def slot(other, dz):
        return me.col((1 - xh) if other else xh, (z + dz + 16) % 8, me.core)

    def pass_on(key, n, half, device):
        piece = rows_ref.at[n, half]
        net.send(key, piece, piece, device)

    near = me.y * 2 + (1 - me.xl)
    halves = (first, second)

    def to_core(key, n):
        net.send(key, rows_ref.at[n], rows_ref.at[n], me.other_core())

    def pass_col(key, row, half, device):
        piece = cols_ref.at[(row + 4) % 8, half]
        net.send(key, piece, piece, device)

    net.send("x1", o_ref.at[first], rows_ref.at[c, first], me.x_far())
    for p, half in enumerate(halves):
        net.send(("permute", p), osh_ref.at[half], cols_ref.at[c % 8, half], target)
    for way in hops:
        net.send(("z2", way, 1), o_ref.at[second], rows_ref.at[c, second], me.at_z(step[way]))
    for way in hops:
        net.send(("z1", way, 1), o_ref.at[first], rows_ref.at[c, first], me.at_z(step[way]))
    net.send(("x2", "own", 0), o_ref.at[second], rows_ref.at[c, second], me.x_far())
    net.send("core_own", o_ref, rows_ref.at[c], me.other_core())
    rows_ref[c] = o_ref[...]

    events = []

    def on(time, key, act=None):
        events.append((time, len(events), key, act))

    onward = {"L": {1: ((3, 2), (2, 1)), 3: ((4, 1),)}, "S": {1: ((2, 1),), 2: ((3, 1),)}}
    arrival = {("L", 1): 4.0, ("L", 2): 8.3, ("L", 3): 8.0, ("L", 4): 12.0}
    arrival.update({("S", 1): 4.1, ("S", 2): 8.1, ("S", 3): 12.1})

    def relay(kind, half, way, t):
        def act():
            n = slot(kind == "z1p", -step[way] * t)
            for later, distance in onward[way].get(t, ()):
                pass_on((kind, way, later), n, half, me.at_z(step[way] * distance))
            if kind == "z2":
                pass_on(("x2", way, t), n, second, me.x_far())
            if kind == "z1":
                to_core(("core", way, t), n)

        return act

    def cross_over():
        for way in hops:
            pass_on(("z1p", way, 1), slot(True, 0), first, me.at_z(step[way]))

    def far(way, t):
        n = slot(True, 0 if t == 0 else -step[way] * t)
        return lambda: to_core(("core_far", way, t), n)

    on(4, "x1", cross_over)
    on(12, ("x2", "own", 0), far("own", 0))
    for t in range(1, 5):
        for way in hops:
            if t <= hops[way]:
                at = arrival[way, t]
                on(at, ("z2", way, t), relay("z2", second, way, t))
                on(at + 1, ("z1", way, t), relay("z1", first, way, t))
                on(at + 4.5, ("z1p", way, t), relay("z1p", first, way, t))
                on(at + 7, ("x2", way, t), far(way, t))
    for p, half in enumerate(halves):
        def spread(p=p, half=half):
            pass_col(("near", p), r, half, me.x_near())
            for d in (1, -1):
                pass_col(("y0", p, d), r, half, me.at_y(d))

        def spread_near(p=p, half=half):
            for d in (2, 1, -1):
                pass_col(("y1", p, d), near, half, me.at_y(d))

        late = 2 * p + COL_LATE
        on(9 + late, ("permute", p), spread)
        on(13 + late, ("near", p), spread_near)
        on(14 + late, ("y0", p, 1), lambda p=p, half=half: pass_col(("y2", p, 1), (r + 6) % 8, half, me.at_y(1)))
    for _, _, key, act in sorted(events, key=lambda e: e[:2]):
        net.wait(key)
        if act is not None:
            act()
    for key, entry in net.copies.items():
        if not entry[1]:
            net.wait(key)


def kernel(
    a_hbm, d_hbm, s_hbm, lag_ref, count_ref, rows_ref, cols_ref,
    a_ref, d_ref, s_ref, in_sem, response, o_scr, osh_scr, a4, dg, sb, rb, sf, rf, send_sem, recv_sem,
):
    me = Place()
    loads = [
        pltpu.make_async_copy(source, target, in_sem.at[n])
        for n, (source, target) in enumerate(((d_hbm, d_ref), (a_hbm, a_ref), (s_hbm, s_ref)))
    ]
    for load in loads:
        load.start()
    greet(
        [me.other_core(), me.x_near(), me.x_far(), me.x_cross(), me.x_far_core(), me.at_z(1), me.at_z(-1)]
        + [me.at_z(2), me.at_z(-2), me.at_y(1), me.at_y(-1), me.at_y(2), me.permuted(), me.permuted_from()]
    )
    net = Net(send_sem, recv_sem)
    for load in loads:
        load.wait()
    response[:, :MARGIN] = jnp.zeros((64, MARGIN), F32)
    reduce_slopes(me, net, a_ref, d_ref, response, a4, dg, sb, rb, sf, rf)
    open_loop(response, s_ref, lag_ref, count_ref, o_scr, osh_scr)
    gather_slopes(me, net, o_scr, osh_scr, rows_ref, cols_ref)
    net.finish()


def gathered(number, frames, interaction, commands, slopes_measured, frame_lag, frame_count):
    kinds = [hop[2] for hop in HOPS.values()]
    n_bf, n_f32 = kinds.count(BF), kinds.count(F32)
    piece = (64, CHUNK)
    copies = 160
    smem = pl.BlockSpec(memory_space=pltpu.SMEM)
    return pl.pallas_call(
        kernel,
        out_shape=(
            jax.ShapeDtypeStruct((32, 64, frames), BF),
            jax.ShapeDtypeStruct((8, 64, frames), BF),
        ),
        in_specs=[pl.BlockSpec(memory_space=pl.ANY)] * 3 + [smem, smem],
        out_specs=(VMEM, VMEM),
        scratch_shapes=[
            pltpu.VMEM((2, 8, 2, 64, 256), BF),
            pltpu.VMEM((128, 256), BF),
            pltpu.VMEM((64, FRAMES), BF),
            pltpu.SemaphoreType.DMA((3,)),
            pltpu.VMEM((64, MARGIN + FRAMES), F32),
            pltpu.VMEM((64, frames), BF),
            pltpu.VMEM((64, frames), BF),
            pltpu.VMEM((3, 8, 64, 256), BF),
            pltpu.VMEM((4, 8, 128, 256), BF),
            pltpu.VMEM((CHUNKS, n_bf) + piece, BF),
            pltpu.VMEM((CHUNKS, n_bf) + piece, BF),
            pltpu.VMEM((CHUNKS, n_f32) + piece, F32),
            pltpu.VMEM((CHUNKS, n_f32) + piece, F32),
            pltpu.SemaphoreType.DMA((copies,)),
            pltpu.SemaphoreType.DMA((copies,)),
        ],
        compiler_params=pltpu.CompilerParams(
            collective_id=number, has_side_effects=True, vmem_limit_bytes=24 * 2**20
        ),
        name=f"open_loop_slopes_{frames}",
    )(interaction.reshape(2, 8, 2, 64, 256), commands, slopes_measured, frame_lag, frame_count)


def covariance(number, *args):
    frames = BOUNDS[number]
    rows, cols = gathered(number, frames, *args)
    tile = lax.dot_general(
        rows.reshape(2048, frames),
        cols.reshape(512, frames),
        (((1,), (1,)), ((), ())),
        preferred_element_type=F32,
    )
    return tile * (1.0 / math.sqrt(FRAMES))


def local(interaction, commands, slopes_measured, frame_lag, frame_count):
    which = sum((frame_count[0] > bound).astype(jnp.int32) for bound in BOUNDS[:-1])
    return lax.switch(
        which,
        [functools.partial(covariance, n) for n in range(len(BOUNDS))],
        interaction, commands, slopes_measured, frame_lag, frame_count,
    )


def solution(mesh):
    return jax.shard_map(
        local,
        mesh=mesh,
        in_specs=(P("rows", "cols"), P("rows", "cols"), P(("rows", "cols"), None), P(), P()),
        out_specs=P("rows", "cols"),
        check_vma=False,
    )
```

```python
import functools
import math

import jax
import jax.numpy as jnp
from jax import lax
from jax.experimental import pallas as pl
from jax.experimental.pallas import tpu as pltpu
from jax.sharding import PartitionSpec as P

FRAMES = 1024
CHUNK = 256
BOUNDS = (512, 640, 768, 896, 1024)
MARGIN = FRAMES // 4
CHUNKS = FRAMES // CHUNK
BF, F32 = jnp.bfloat16, jnp.float32
VMEM = pl.BlockSpec(memory_space=pltpu.VMEM)
Y_ORDER = (0, 1, 3, 2)
HOPS = {
    "L4": (4, 2, BF, 1, ()),
    "L3": (3, 1, BF, 1, ()),
    "S3": (-3, -2, BF, 1, ()),
    "S2": (-2, -1, BF, 1, ()),
    "L2": (2, 1, BF, 2, ("L4", "L3")),
    "S1": (-1, -1, F32, 2, ("S3", "S2")),
    "L1": (1, 1, F32, 3, ("L2",)),
}
STAGES = 3
A_ORDER = (4, 3, -3, -2, 2, -1, 1, 0)
CHUNK_START = (9.0, 11.2, 11.3, 14.0)
HOP_TIME = 4.0
COL_LATE = -5.0


class Place:
    def __init__(self):
        self.r = lax.axis_index("rows")
        self.c = lax.axis_index("cols")
        self.y, self.xl = self.r // 2, self.r % 2
        self.xh, self.z, self.core = self.c // 16, (self.c // 2) % 8, self.c % 2
        self.sign = 1 - 2 * self.core

    def col(self, xh, z, core):
        return xh * 16 + z * 2 + core

    def at_z(self, dz):
        return self.r, self.col(self.xh, (self.z + dz + 16) % 8, self.core)

    def at_y(self, dy):
        return (self.r + 2 * dy + 8) % 8, self.c

    def x_far(self):
        return self.r, (self.c + 16) % 32

    def permuted(self):
        return (self.c + 4) % 8, self.r * 4 + self.c // 8

    def permuted_from(self):
        return self.c // 4, (self.c % 4) * 8 + (self.r + 4) % 8

    def x_far_core(self):
        return self.r, self.col(1 - self.xh, self.z, 1 - self.core)

    def x_cross(self):
        return self.y * 2 + (1 - self.xl), (self.c + 16) % 32

    def x_near(self):
        return self.y * 2 + (1 - self.xl), self.c

    def other_core(self):
        return self.r, self.c + self.sign


class Net:
    def __init__(self, send_sem, recv_sem):
        self.send_sem, self.recv_sem = send_sem, recv_sem
        self.copies = {}
        self.used = 0

    def reserve(self, count):
        self.used += count
        return self.used - count

    def send(self, key, src, dst, device):
        n = self.reserve(1)
        copy = pltpu.make_async_remote_copy(
            src_ref=src,
            dst_ref=dst,
            send_sem=self.send_sem.at[n],
            recv_sem=self.recv_sem.at[n],
            device_id=device,
            device_id_type=pl.DeviceIdType.MESH,
        )
        copy.start()
        self.copies[key] = [copy, False]

    def wait(self, key):
        entry = self.copies[key]
        assert not entry[1]
        entry[0].wait_recv()
        entry[1] = True

    def finish(self):
        for copy, received in self.copies.values():
            assert received
            copy.wait_send()


def greet(devices):
    barrier = pltpu.get_barrier_semaphore()
    for device in devices:
        pl.semaphore_signal(barrier, inc=1, device_id=device, device_id_type=pl.DeviceIdType.MESH)
    pl.semaphore_wait(barrier, len(devices))


def reduce_slopes(me, net, frames, a_ref, d_ref, response, a4, dg, sb, rb, sf, rf):
    r, z, xh, core, sign = me.r, me.z, me.xh, me.core, me.sign
    near = me.y * 2 + (1 - me.xl)

    def place(ahead, sgn):
        return (z + sgn * ahead + 16) % 8

    net.send("d_far", d_ref, dg.at[2, r], me.x_far())
    net.send("d_near", d_ref, dg.at[0, r], me.x_near())
    net.send("d_cross", d_ref, dg.at[2, r], me.x_cross())
    net.send(("core", "d", 0), d_ref, dg.at[1, r], me.other_core())
    for o in (2, 1, 3):
        net.send(("d", o), d_ref, dg.at[0, r], me.at_y(-o))
    net.send("a_core", a_ref.at[xh, :, 1 - core], a4.at[0], me.other_core())

    def send_rows(places):
        for ahead in places:
            n = place(ahead, sign)
            net.send(("a_far", ahead), a_ref.at[1 - xh, n, core], a4.at[1, n], me.x_far())
            n = place(ahead, -sign)
            net.send(("a_cross", ahead), a_ref.at[1 - xh, n, 1 - core], a4.at[2, n], me.x_far_core())

    send_rows(A_ORDER[:4])
    dg[0, r] = d_ref[...]
    def y_of(f):
        return (me.y + Y_ORDER[f]) % 4

    pieces_of = (("d", 0, me.xl), ("d_near", 0, 1 - me.xl), ("d_cross", 2, 1 - me.xl), ("d_far", 2, me.xl))

    def from_x(key, k, row):
        def act():
            net.wait(key)
            piece = dg.at[k, row]
            for o in (1, 3):
                net.send((key, o), piece, piece, me.at_y(-o))
            net.send(("core", key, 0), piece, dg.at[k + 1, row], me.other_core())

        return act

    def from_y(key, k, side, o):
        def act():
            net.wait((key, o))
            row = (me.y + o) % 4 * 2 + side
            piece = dg.at[k, row]
            if (o, key) == (2, "d"):
                net.send(("d_far", 2), piece, dg.at[2, row], me.x_far())
                net.send(("d_near", 2), piece, piece, me.x_near())
                net.send(("d_cross", 2), piece, dg.at[2, row], me.x_cross())
                send_rows(A_ORDER[4:])
            net.send(("core", key, o), piece, dg.at[k + 1, row], me.other_core())

        return act

    def commands_in(f):
        for key, _, _ in pieces_of:
            net.wait(("core", key, Y_ORDER[f]))
        if f == 0:
            net.wait("a_core")

    arrived = set()

    def rows_in(places):
        for ahead in places:
            if ahead not in arrived:
                arrived.add(ahead)
                net.wait(("a_far", ahead))
                net.wait(("a_cross", ahead))

    def product(f, places):
        owners = [place(ahead, sign) for ahead in places]
        total = None
        for k in range(4):
            if k == 0:
                rows = [a_ref[xh, n, core] for n in owners]
            else:
                rows = [a4[k - 1, n] for n in owners]
            part = lax.dot_general(
                jnp.concatenate(rows, axis=0),
                dg[k, pl.ds(y_of(f) * 2, 2)].reshape(CHUNK, 256),
                (((1,), (1,)), ((), ())),
                preferred_element_type=F32,
            )
            total = part if total is None else total + part
        return [total[i * 64 : (i + 1) * 64] for i in range(len(places))]

    slots = {}
    for name, (_, _, kind, _, _) in HOPS.items():
        slots[name] = (kind, sum(1 for k, _ in slots.values() if k is kind))

    def buffer(f, name, sending):
        kind, n = slots[name]
        if kind is BF:
            return (sb if sending else rb).at[f, n]
        return (sf if sending else rf).at[f, n]

    partner = {to: me.at_z(sign * to) for _, to, _, _, _ in HOPS.values()}
    first = net.reserve(CHUNKS * len(HOPS))

    def hop_copy(f, name):
        n = first + f * len(HOPS) + list(HOPS).index(name)
        return pltpu.make_async_remote_copy(
            src_ref=buffer(f, name, True),
            dst_ref=buffer(f, name, False),
            send_sem=net.send_sem.at[n],
            recv_sem=net.recv_sem.at[n],
            device_id=partner[HOPS[name][1]],
            device_id_type=pl.DeviceIdType.MESH,
        )

    def if_needed(f, act):
        if frames == FRAMES:
            act()
        else:
            pl.when(y_of(f) < -(-frames // CHUNK))(act)

    def plus_received(f, value, names):
        for name in names:
            hop_copy(f, name).wait_recv()
            value += buffer(f, name, False)[...].astype(F32)
        return value

    def stage(f, number):
        if number == 1:
            commands_in(f)
        names = [name for name, hop in HOPS.items() if hop[3] == number]
        places = [HOPS[name][0] for name in names]
        rows_in(places)

        def act():
            for name, value in zip(names, product(f, places)):
                _, _, kind, _, received = HOPS[name]
                buffer(f, name, True)[...] = plus_received(f, value, received).astype(kind)
                hop_copy(f, name).start()

        if_needed(f, act)

    def total(f):
        rows_in([0])

        def act():
            (value,) = product(f, [0])
            value = plus_received(f, value, ("S1", "L1"))
            start = pl.multiple_of(MARGIN + y_of(f) * CHUNK, CHUNK)
            response[:, pl.ds(start, CHUNK)] = value
            for name in HOPS:
                hop_copy(f, name).wait_send()

        if_needed(f, act)

    events = []

    def on(time, act):
        events.append((time, len(events), act))

    on(4.0, from_x("d_near", 0, near))
    on(4.2, from_x("d_cross", 2, near))
    on(6.0, from_x("d_far", 2, r))
    for o, times in ((1, (4.5, 8.2, 9.0, 11.0)), (3, (4.5, 8.2, 9.0, 11.0)), (2, (5.0, 12.2, 12.4, 13.5))):
        for time, (key, k, side) in zip(times, pieces_of):
            on(time, from_y(key, k, side, o))
    for f, begin in enumerate(CHUNK_START):
        for number in range(1, STAGES + 1):
            on(begin + HOP_TIME * (number - 1), lambda f=f, number=number: stage(f, number))
        on(begin + HOP_TIME * STAGES, lambda f=f: total(f))
    for _, _, act in sorted(events, key=lambda e: e[:2]):
        act()


def open_loop(response, s_ref, lag_ref, count_ref, o_ref, osh_ref):
    frames = o_ref.shape[1]
    window = response[:, : MARGIN + frames]
    lag = jnp.full(window.shape, lag_ref[0], jnp.int32)
    for bit in range(MARGIN.bit_length()):
        moved = pltpu.roll(window, 1 << bit, 1)
        window = jnp.where((lag & (1 << bit)) != 0, moved, window)
    summed = window[:, MARGIN:] + s_ref[:, :frames].astype(F32)
    frame = lax.broadcasted_iota(jnp.int32, summed.shape, 1)
    count = jnp.full(summed.shape, count_ref[0], jnp.int32)
    value = jnp.where(frame < count, summed, 0.0).astype(BF)
    o_ref[...] = value
    later = pltpu.roll(value.astype(F32), 1, 1)
    osh_ref[...] = jnp.where(frame == 0, 0.0, later).astype(BF)


def gather_slopes(me, net, o_ref, osh_ref, rows_ref, cols_ref):
    r, c, z, xh = me.r, me.c, me.z, me.xh
    target = me.permuted()
    first, second = pl.ds(0, 32), pl.ds(32, 32)
    hops = {"L": 4, "S": 3}
    step = {"L": me.sign, "S": -me.sign}

    def slot(other, dz):
        return me.col((1 - xh) if other else xh, (z + dz + 16) % 8, me.core)

    def pass_on(key, n, half, device):
        piece = rows_ref.at[n, half]
        net.send(key, piece, piece, device)

    near = me.y * 2 + (1 - me.xl)
    halves = (first, second)

    def to_core(key, n):
        net.send(key, rows_ref.at[n], rows_ref.at[n], me.other_core())

    def pass_col(key, row, half, device):
        piece = cols_ref.at[(row + 4) % 8, half]
        net.send(key, piece, piece, device)

    net.send("x1", o_ref.at[first], rows_ref.at[c, first], me.x_far())
    for p, half in enumerate(halves):
        net.send(("permute", p), osh_ref.at[half], cols_ref.at[c % 8, half], target)
    for way in hops:
        net.send(("z2", way, 1), o_ref.at[second], rows_ref.at[c, second], me.at_z(step[way]))
    for way in hops:
        net.send(("z1", way, 1), o_ref.at[first], rows_ref.at[c, first], me.at_z(step[way]))
    net.send(("x2", "own", 0), o_ref.at[second], rows_ref.at[c, second], me.x_far())
    net.send("core_own", o_ref, rows_ref.at[c], me.other_core())
    rows_ref[c] = o_ref[...]

    events = []

    def on(time, key, act=None):
        events.append((time, len(events), key, act))

    onward = {"L": {1: ((3, 2), (2, 1)), 3: ((4, 1),)}, "S": {1: ((2, 1),), 2: ((3, 1),)}}
    arrival = {("L", 1): 4.0, ("L", 2): 8.3, ("L", 3): 8.0, ("L", 4): 12.0}
    arrival.update({("S", 1): 4.1, ("S", 2): 8.1, ("S", 3): 12.1})

    def relay(kind, half, way, t):
        def act():
            n = slot(kind == "z1p", -step[way] * t)
            for later, distance in onward[way].get(t, ()):
                pass_on((kind, way, later), n, half, me.at_z(step[way] * distance))
            if kind == "z2":
                pass_on(("x2", way, t), n, second, me.x_far())
            if kind == "z1":
                to_core(("core", way, t), n)

        return act

    def cross_over():
        for way in hops:
            pass_on(("z1p", way, 1), slot(True, 0), first, me.at_z(step[way]))

    def far(way, t):
        n = slot(True, 0 if t == 0 else -step[way] * t)
        return lambda: to_core(("core_far", way, t), n)

    on(4, "x1", cross_over)
    on(12, ("x2", "own", 0), far("own", 0))
    for t in range(1, 5):
        for way in hops:
            if t <= hops[way]:
                at = arrival[way, t]
                on(at, ("z2", way, t), relay("z2", second, way, t))
                on(at + 1, ("z1", way, t), relay("z1", first, way, t))
                on(at + 4.5, ("z1p", way, t), relay("z1p", first, way, t))
                on(at + 7, ("x2", way, t), far(way, t))
    for p, half in enumerate(halves):
        def spread(p=p, half=half):
            pass_col(("near", p), r, half, me.x_near())
            for d in (1, -1):
                pass_col(("y0", p, d), r, half, me.at_y(d))

        def spread_near(p=p, half=half):
            for d in (2, 1, -1):
                pass_col(("y1", p, d), near, half, me.at_y(d))

        late = 2 * p + COL_LATE
        on(9 + late, ("permute", p), spread)
        on(13 + late, ("near", p), spread_near)
        on(14 + late, ("y0", p, 1), lambda p=p, half=half: pass_col(("y2", p, 1), (r + 6) % 8, half, me.at_y(1)))
    for _, _, key, act in sorted(events, key=lambda e: e[:2]):
        net.wait(key)
        if act is not None:
            act()
    for key, entry in net.copies.items():
        if not entry[1]:
            net.wait(key)


def kernel(
    a_hbm, d_hbm, s_hbm, lag_ref, count_ref, rows_ref, cols_ref,
    a_ref, d_ref, s_ref, in_sem, response, o_scr, osh_scr, a4, dg, sb, rb, sf, rf, send_sem, recv_sem,
):
    me = Place()
    loads = [
        pltpu.make_async_copy(source, target, in_sem.at[n])
        for n, (source, target) in enumerate(((d_hbm, d_ref), (a_hbm, a_ref), (s_hbm, s_ref)))
    ]
    for load in loads:
        load.start()
    greet(
        [me.other_core(), me.x_near(), me.x_far(), me.x_cross(), me.x_far_core(), me.at_z(1), me.at_z(-1)]
        + [me.at_z(2), me.at_z(-2), me.at_y(1), me.at_y(-1), me.at_y(2), me.permuted(), me.permuted_from()]
    )
    net = Net(send_sem, recv_sem)
    for load in loads:
        load.wait()
    response[...] = jnp.zeros_like(response)
    reduce_slopes(me, net, o_scr.shape[1], a_ref, d_ref, response, a4, dg, sb, rb, sf, rf)
    open_loop(response, s_ref, lag_ref, count_ref, o_scr, osh_scr)
    gather_slopes(me, net, o_scr, osh_scr, rows_ref, cols_ref)
    net.finish()


def gathered(number, frames, interaction, commands, slopes_measured, frame_lag, frame_count):
    kinds = [hop[2] for hop in HOPS.values()]
    n_bf, n_f32 = kinds.count(BF), kinds.count(F32)
    piece = (64, CHUNK)
    copies = 160
    smem = pl.BlockSpec(memory_space=pltpu.SMEM)
    return pl.pallas_call(
        kernel,
        out_shape=(
            jax.ShapeDtypeStruct((32, 64, frames), BF),
            jax.ShapeDtypeStruct((8, 64, frames), BF),
        ),
        in_specs=[pl.BlockSpec(memory_space=pl.ANY)] * 3 + [smem, smem],
        out_specs=(VMEM, VMEM),
        scratch_shapes=[
            pltpu.VMEM((2, 8, 2, 64, 256), BF),
            pltpu.VMEM((128, 256), BF),
            pltpu.VMEM((64, FRAMES), BF),
            pltpu.SemaphoreType.DMA((3,)),
            pltpu.VMEM((64, MARGIN + FRAMES), F32),
            pltpu.VMEM((64, frames), BF),
            pltpu.VMEM((64, frames), BF),
            pltpu.VMEM((3, 8, 64, 256), BF),
            pltpu.VMEM((4, 8, 128, 256), BF),
            pltpu.VMEM((CHUNKS, n_bf) + piece, BF),
            pltpu.VMEM((CHUNKS, n_bf) + piece, BF),
            pltpu.VMEM((CHUNKS, n_f32) + piece, F32),
            pltpu.VMEM((CHUNKS, n_f32) + piece, F32),
            pltpu.SemaphoreType.DMA((copies,)),
            pltpu.SemaphoreType.DMA((copies,)),
        ],
        compiler_params=pltpu.CompilerParams(
            collective_id=number, has_side_effects=True, vmem_limit_bytes=24 * 2**20
        ),
        name=f"open_loop_slopes_{frames}",
    )(interaction.reshape(2, 8, 2, 64, 256), commands, slopes_measured, frame_lag, frame_count)


def covariance(number, *args):
    frames = BOUNDS[number]
    rows, cols = gathered(number, frames, *args)
    tile = lax.dot_general(
        rows.reshape(2048, frames),
        cols.reshape(512, frames),
        (((1,), (1,)), ((), ())),
        preferred_element_type=F32,
    )
    return tile * (1.0 / math.sqrt(FRAMES))


def local(interaction, commands, slopes_measured, frame_lag, frame_count):
    which = sum((frame_count[0] > bound).astype(jnp.int32) for bound in BOUNDS[:-1])
    return lax.switch(
        which,
        [functools.partial(covariance, n) for n in range(len(BOUNDS))],
        interaction, commands, slopes_measured, frame_lag, frame_count,
    )


def solution(mesh):
    return jax.shard_map(
        local,
        mesh=mesh,
        in_specs=(P("rows", "cols"), P("rows", "cols"), P(("rows", "cols"), None), P(), P()),
        out_specs=P("rows", "cols"),
        check_vma=False,
    )
```

```python
import functools
import math

import jax
import jax.numpy as jnp
from jax import lax
from jax.experimental import pallas as pl
from jax.experimental.pallas import tpu as pltpu
from jax.sharding import PartitionSpec as P

FRAMES = 1024
CHUNK = 256
BOUNDS = (512, 640, 768, 896, 1024)
MARGIN = FRAMES // 4
CHUNKS = FRAMES // CHUNK
BF, F32 = jnp.bfloat16, jnp.float32
VMEM = pl.BlockSpec(memory_space=pltpu.VMEM)
Y_ORDER = (0, 1, 3, 2)
HOPS = {
    "L4": (4, 2, BF, 1, ()),
    "L3": (3, 1, BF, 1, ()),
    "S3": (-3, -2, BF, 1, ()),
    "S2": (-2, -1, BF, 1, ()),
    "L2": (2, 1, BF, 2, ("L4", "L3")),
    "S1": (-1, -1, F32, 2, ("S3", "S2")),
    "L1": (1, 1, F32, 3, ("L2",)),
}
STAGES = 3
A_ORDER = (4, 3, -3, -2, 2, -1, 1, 0)
CHUNK_START = (9.0, 11.2, 11.3, 14.0)
HOP_TIME = 4.0
COL_LATE = -5.0


class Place:
    def __init__(self):
        self.r = lax.axis_index("rows")
        self.c = lax.axis_index("cols")
        self.y, self.xl = self.r // 2, self.r % 2
        self.xh, self.z, self.core = self.c // 16, (self.c // 2) % 8, self.c % 2
        self.sign = 1 - 2 * self.core

    def col(self, xh, z, core):
        return xh * 16 + z * 2 + core

    def at_z(self, dz):
        return self.r, self.col(self.xh, (self.z + dz + 16) % 8, self.core)

    def at_y(self, dy):
        return (self.r + 2 * dy + 8) % 8, self.c

    def x_far(self):
        return self.r, (self.c + 16) % 32

    def permuted(self):
        return (self.c + 4) % 8, self.r * 4 + self.c // 8

    def permuted_from(self):
        return self.c // 4, (self.c % 4) * 8 + (self.r + 4) % 8

    def x_far_core(self):
        return self.r, self.col(1 - self.xh, self.z, 1 - self.core)

    def x_cross(self):
        return self.y * 2 + (1 - self.xl), (self.c + 16) % 32

    def x_near(self):
        return self.y * 2 + (1 - self.xl), self.c

    def other_core(self):
        return self.r, self.c + self.sign


class Net:
    def __init__(self, send_sem, recv_sem):
        self.send_sem, self.recv_sem = send_sem, recv_sem
        self.copies = {}
        self.used = 0

    def reserve(self, count):
        self.used += count
        return self.used - count

    def send(self, key, src, dst, device):
        n = self.reserve(1)
        copy = pltpu.make_async_remote_copy(
            src_ref=src,
            dst_ref=dst,
            send_sem=self.send_sem.at[n],
            recv_sem=self.recv_sem.at[n],
            device_id=device,
            device_id_type=pl.DeviceIdType.MESH,
        )
        copy.start()
        self.copies[key] = [copy, False]

    def wait(self, key):
        entry = self.copies[key]
        assert not entry[1]
        entry[0].wait_recv()
        entry[1] = True

    def finish(self):
        for copy, received in self.copies.values():
            assert received
            copy.wait_send()


def greet(devices):
    barrier = pltpu.get_barrier_semaphore()
    for device in devices:
        pl.semaphore_signal(barrier, inc=1, device_id=device, device_id_type=pl.DeviceIdType.MESH)
    pl.semaphore_wait(barrier, len(devices))


def reduce_slopes(me, net, frames, a_ref, d_ref, response, a4, dg, sb, rb, sf, rf):
    r, z, xh, core, sign = me.r, me.z, me.xh, me.core, me.sign
    near = me.y * 2 + (1 - me.xl)

    def place(ahead, sgn):
        return (z + sgn * ahead + 16) % 8

    net.send("d_far", d_ref, dg.at[2, r], me.x_far())
    net.send("d_near", d_ref, dg.at[0, r], me.x_near())
    net.send("d_cross", d_ref, dg.at[2, r], me.x_cross())
    net.send(("core", "d", 0), d_ref, dg.at[1, r], me.other_core())
    for o in (2, 1, 3):
        net.send(("d", o), d_ref, dg.at[0, r], me.at_y(-o))
    net.send("a_core", a_ref.at[xh, :, 1 - core], a4.at[0], me.other_core())

    def send_rows(places):
        for ahead in places:
            n = place(ahead, sign)
            net.send(("a_far", ahead), a_ref.at[1 - xh, n, core], a4.at[1, n], me.x_far())
            n = place(ahead, -sign)
            net.send(("a_cross", ahead), a_ref.at[1 - xh, n, 1 - core], a4.at[2, n], me.x_far_core())

    send_rows(A_ORDER[:4])
    dg[0, r] = d_ref[...]
    def y_of(f):
        return (me.y + Y_ORDER[f]) % 4

    pieces_of = (("d", 0, me.xl), ("d_near", 0, 1 - me.xl), ("d_cross", 2, 1 - me.xl), ("d_far", 2, me.xl))

    def from_x(key, k, row):
        def act():
            net.wait(key)
            piece = dg.at[k, row]
            for o in (1, 3):
                net.send((key, o), piece, piece, me.at_y(-o))
            net.send(("core", key, 0), piece, dg.at[k + 1, row], me.other_core())

        return act

    def from_y(key, k, side, o):
        def act():
            net.wait((key, o))
            row = (me.y + o) % 4 * 2 + side
            piece = dg.at[k, row]
            if (o, key) == (2, "d"):
                net.send(("d_far", 2), piece, dg.at[2, row], me.x_far())
                net.send(("d_near", 2), piece, piece, me.x_near())
                net.send(("d_cross", 2), piece, dg.at[2, row], me.x_cross())
                send_rows(A_ORDER[4:])
            net.send(("core", key, o), piece, dg.at[k + 1, row], me.other_core())

        return act

    def commands_in(f):
        for key, _, _ in pieces_of:
            net.wait(("core", key, Y_ORDER[f]))
        if f == 0:
            net.wait("a_core")

    arrived = set()

    def rows_in(places):
        for ahead in places:
            if ahead not in arrived:
                arrived.add(ahead)
                net.wait(("a_far", ahead))
                net.wait(("a_cross", ahead))

    def product(f, places):
        owners = [place(ahead, sign) for ahead in places]
        total = None
        for k in range(4):
            if k == 0:
                rows = [a_ref[xh, n, core] for n in owners]
            else:
                rows = [a4[k - 1, n] for n in owners]
            part = lax.dot_general(
                jnp.concatenate(rows, axis=0),
                dg[k, pl.ds(y_of(f) * 2, 2)].reshape(CHUNK, 256),
                (((1,), (1,)), ((), ())),
                preferred_element_type=F32,
            )
            total = part if total is None else total + part
        return [total[i * 64 : (i + 1) * 64] for i in range(len(places))]

    slots = {}
    for name, (_, _, kind, _, _) in HOPS.items():
        slots[name] = (kind, sum(1 for k, _ in slots.values() if k is kind))

    def buffer(f, name, sending):
        kind, n = slots[name]
        if kind is BF:
            return (sb if sending else rb).at[f, n]
        return (sf if sending else rf).at[f, n]

    partner = {to: me.at_z(sign * to) for _, to, _, _, _ in HOPS.values()}
    first = net.reserve(CHUNKS * len(HOPS))

    def hop_copy(f, name):
        n = first + f * len(HOPS) + list(HOPS).index(name)
        return pltpu.make_async_remote_copy(
            src_ref=buffer(f, name, True),
            dst_ref=buffer(f, name, False),
            send_sem=net.send_sem.at[n],
            recv_sem=net.recv_sem.at[n],
            device_id=partner[HOPS[name][1]],
            device_id_type=pl.DeviceIdType.MESH,
        )

    def if_needed(f, act):
        if frames == FRAMES:
            act()
        else:
            pl.when(y_of(f) < -(-frames // CHUNK))(act)

    def plus_received(f, value, names):
        for name in names:
            hop_copy(f, name).wait_recv()
            value += buffer(f, name, False)[...].astype(F32)
        return value

    def stage(f, number):
        if number == 1:
            commands_in(f)
        names = [name for name, hop in HOPS.items() if hop[3] == number]
        places = [HOPS[name][0] for name in names]
        rows_in(places)

        def act():
            for name, value in zip(names, product(f, places)):
                _, _, kind, _, received = HOPS[name]
                buffer(f, name, True)[...] = plus_received(f, value, received).astype(kind)
                hop_copy(f, name).start()

        if_needed(f, act)

    def total(f):
        rows_in([0])

        def act():
            (value,) = product(f, [0])
            value = plus_received(f, value, ("S1", "L1"))
            start = pl.multiple_of(MARGIN + y_of(f) * CHUNK, CHUNK)
            response[:, pl.ds(start, CHUNK)] = value
            for name in HOPS:
                hop_copy(f, name).wait_send()

        if_needed(f, act)

    events = []

    def on(time, act):
        events.append((time, len(events), act))

    on(4.0, from_x("d_near", 0, near))
    on(4.2, from_x("d_cross", 2, near))
    on(6.0, from_x("d_far", 2, r))
    for o, times in ((1, (4.5, 8.2, 9.0, 11.0)), (3, (4.5, 8.2, 9.0, 11.0)), (2, (5.0, 12.2, 12.4, 13.5))):
        for time, (key, k, side) in zip(times, pieces_of):
            on(time, from_y(key, k, side, o))
    for f, begin in enumerate(CHUNK_START):
        for number in range(1, STAGES + 1):
            on(begin + HOP_TIME * (number - 1), lambda f=f, number=number: stage(f, number))
        on(begin + HOP_TIME * STAGES, lambda f=f: total(f))
    for _, _, act in sorted(events, key=lambda e: e[:2]):
        act()


def open_loop(response, s_ref, lag_ref, count_ref, o_ref, osh_ref):
    frames = o_ref.shape[1]
    window = response[:, : MARGIN + frames]
    lag = jnp.full(window.shape, lag_ref[0], jnp.int32)
    for bit in range(MARGIN.bit_length()):
        moved = pltpu.roll(window, 1 << bit, 1)
        window = jnp.where((lag & (1 << bit)) != 0, moved, window)
    summed = window[:, MARGIN:] + s_ref[:, :frames].astype(F32)
    frame = lax.broadcasted_iota(jnp.int32, summed.shape, 1)
    count = jnp.full(summed.shape, count_ref[0], jnp.int32)
    value = jnp.where(frame < count, summed, 0.0).astype(BF)
    o_ref[...] = value
    later = pltpu.roll(value.astype(F32), 1, 1)
    osh_ref[...] = jnp.where(frame == 0, 0.0, later).astype(BF)


def gather_slopes(me, net, o_ref, osh_ref, rows_ref, cols_ref):
    r, c, z, xh = me.r, me.c, me.z, me.xh
    target = me.permuted()
    first, second = pl.ds(0, 32), pl.ds(32, 32)
    hops = {"L": 4, "S": 3}
    step = {"L": me.sign, "S": -me.sign}
    short = o_ref.shape[1] <= 640
    opening = [("L", 1), ("S", 1)] + [("L", 2)] * short

    def slot(other, dz):
        return me.col((1 - xh) if other else xh, (z + dz + 16) % 8, me.core)

    def pass_on(key, n, half, device):
        piece = rows_ref.at[n, half]
        net.send(key, piece, piece, device)

    near = me.y * 2 + (1 - me.xl)
    halves = (first, second)

    def to_core(key, n):
        net.send(key, rows_ref.at[n], rows_ref.at[n], me.other_core())

    def pass_col(key, row, half, device):
        piece = cols_ref.at[(row + 4) % 8, half]
        net.send(key, piece, piece, device)

    net.send("x1", o_ref.at[first], rows_ref.at[c, first], me.x_far())
    for p, half in enumerate(halves):
        net.send(("permute", p), osh_ref.at[half], cols_ref.at[c % 8, half], target)
    for kind, half in (("z2", second), ("z1", first)):
        for way, t in opening:
            net.send((kind, way, t), o_ref.at[half], rows_ref.at[c, half], me.at_z(step[way] * t))
    net.send(("x2", "own", 0), o_ref.at[second], rows_ref.at[c, second], me.x_far())
    net.send("core_own", o_ref, rows_ref.at[c], me.other_core())
    rows_ref[c] = o_ref[...]

    events = []

    def on(time, key, act=None):
        events.append((time, len(events), key, act))

    onward = {"L": {1: ((3, 2), (2, 1)), 3: ((4, 1),)}, "S": {1: ((2, 1),), 2: ((3, 1),)}}
    arrival = {("L", 1): 4.0, ("L", 2): 8.3, ("L", 3): 8.0, ("L", 4): 12.0}
    arrival.update({("S", 1): 4.1, ("S", 2): 8.1, ("S", 3): 12.1})

    if short:
        onward = {"L": {2: ((4, 2), (3, 1))}, "S": {1: ((3, 2), (2, 1))}}
        arrival.update({("L", 2): 5.0, ("L", 3): 8.5, ("L", 4): 9.0, ("S", 3): 8.9})

    def relay(kind, half, way, t):
        def act():
            n = slot(kind == "z1p", -step[way] * t)
            for later, distance in onward[way].get(t, ()):
                pass_on((kind, way, later), n, half, me.at_z(step[way] * distance))
            if kind == "z2":
                pass_on(("x2", way, t), n, second, me.x_far())
            if kind == "z1":
                to_core(("core", way, t), n)

        return act

    def cross_over():
        for way, t in opening:
            pass_on(("z1p", way, t), slot(True, 0), first, me.at_z(step[way] * t))

    def far(way, t):
        n = slot(True, 0 if t == 0 else -step[way] * t)
        return lambda: to_core(("core_far", way, t), n)

    on(4, "x1", cross_over)
    on(12, ("x2", "own", 0), far("own", 0))
    for t in range(1, 5):
        for way in hops:
            if t <= hops[way]:
                at = arrival[way, t]
                on(at, ("z2", way, t), relay("z2", second, way, t))
                on(at + 1, ("z1", way, t), relay("z1", first, way, t))
                on(at + 4.5, ("z1p", way, t), relay("z1p", first, way, t))
                on(at + 7, ("x2", way, t), far(way, t))
    for p, half in enumerate(halves):
        def spread(p=p, half=half):
            pass_col(("near", p), r, half, me.x_near())
            for d in (1, -1):
                pass_col(("y0", p, d), r, half, me.at_y(d))

        def spread_near(p=p, half=half):
            for d in (2, 1, -1):
                pass_col(("y1", p, d), near, half, me.at_y(d))

        late = 2 * p + COL_LATE
        on(9 + late, ("permute", p), spread)
        on(13 + late, ("near", p), spread_near)
        on(14 + late, ("y0", p, 1), lambda p=p, half=half: pass_col(("y2", p, 1), (r + 6) % 8, half, me.at_y(1)))
    for _, _, key, act in sorted(events, key=lambda e: e[:2]):
        net.wait(key)
        if act is not None:
            act()
    for key, entry in net.copies.items():
        if not entry[1]:
            net.wait(key)


def kernel(
    a_hbm, d_hbm, s_hbm, lag_ref, count_ref, rows_ref, cols_ref,
    a_ref, d_ref, s_ref, in_sem, response, o_scr, osh_scr, a4, dg, sb, rb, sf, rf, send_sem, recv_sem,
):
    me = Place()
    loads = [
        pltpu.make_async_copy(source, target, in_sem.at[n])
        for n, (source, target) in enumerate(((d_hbm, d_ref), (a_hbm, a_ref), (s_hbm, s_ref)))
    ]
    for load in loads:
        load.start()
    greet(
        [me.other_core(), me.x_near(), me.x_far(), me.x_cross(), me.x_far_core(), me.at_z(1), me.at_z(-1)]
        + [me.at_z(2), me.at_z(-2), me.at_y(1), me.at_y(-1), me.at_y(2), me.permuted(), me.permuted_from()]
    )
    net = Net(send_sem, recv_sem)
    for load in loads:
        load.wait()
    response[...] = jnp.zeros_like(response)
    reduce_slopes(me, net, o_scr.shape[1], a_ref, d_ref, response, a4, dg, sb, rb, sf, rf)
    open_loop(response, s_ref, lag_ref, count_ref, o_scr, osh_scr)
    gather_slopes(me, net, o_scr, osh_scr, rows_ref, cols_ref)
    net.finish()


def gathered(number, frames, interaction, commands, slopes_measured, frame_lag, frame_count):
    kinds = [hop[2] for hop in HOPS.values()]
    n_bf, n_f32 = kinds.count(BF), kinds.count(F32)
    piece = (64, CHUNK)
    copies = 160
    smem = pl.BlockSpec(memory_space=pltpu.SMEM)
    return pl.pallas_call(
        kernel,
        out_shape=(
            jax.ShapeDtypeStruct((32, 64, frames), BF),
            jax.ShapeDtypeStruct((8, 64, frames), BF),
        ),
        in_specs=[pl.BlockSpec(memory_space=pl.ANY)] * 3 + [smem, smem],
        out_specs=(VMEM, VMEM),
        scratch_shapes=[
            pltpu.VMEM((2, 8, 2, 64, 256), BF),
            pltpu.VMEM((128, 256), BF),
            pltpu.VMEM((64, FRAMES), BF),
            pltpu.SemaphoreType.DMA((3,)),
            pltpu.VMEM((64, MARGIN + FRAMES), F32),
            pltpu.VMEM((64, frames), BF),
            pltpu.VMEM((64, frames), BF),
            pltpu.VMEM((3, 8, 64, 256), BF),
            pltpu.VMEM((4, 8, 128, 256), BF),
            pltpu.VMEM((CHUNKS, n_bf) + piece, BF),
            pltpu.VMEM((CHUNKS, n_bf) + piece, BF),
            pltpu.VMEM((CHUNKS, n_f32) + piece, F32),
            pltpu.VMEM((CHUNKS, n_f32) + piece, F32),
            pltpu.SemaphoreType.DMA((copies,)),
            pltpu.SemaphoreType.DMA((copies,)),
        ],
        compiler_params=pltpu.CompilerParams(
            collective_id=number, has_side_effects=True, vmem_limit_bytes=24 * 2**20
        ),
        name=f"open_loop_slopes_{frames}",
    )(interaction.reshape(2, 8, 2, 64, 256), commands, slopes_measured, frame_lag, frame_count)


def covariance(number, *args):
    frames = BOUNDS[number]
    rows, cols = gathered(number, frames, *args)
    tile = lax.dot_general(
        rows.reshape(2048, frames),
        cols.reshape(512, frames),
        (((1,), (1,)), ((), ())),
        preferred_element_type=F32,
    )
    return tile * (1.0 / math.sqrt(FRAMES))


def local(interaction, commands, slopes_measured, frame_lag, frame_count):
    which = sum((frame_count[0] > bound).astype(jnp.int32) for bound in BOUNDS[:-1])
    return lax.switch(
        which,
        [functools.partial(covariance, n) for n in range(len(BOUNDS))],
        interaction, commands, slopes_measured, frame_lag, frame_count,
    )


def solution(mesh):
    return jax.shard_map(
        local,
        mesh=mesh,
        in_specs=(P("rows", "cols"), P("rows", "cols"), P(("rows", "cols"), None), P(), P()),
        out_specs=P("rows", "cols"),
        check_vma=False,
    )
```
